256 devices in a mesh: pulse: 16 (over z, core), range: 16 (over x, y).
Axes of the slice: x: 4, y: 4, z: 8, core: 2. Of those that a mesh axis runs over, the one named last changes fastest.
Arguments:
- pulse_data: bfloat16 [2, 16384, 4096], P(None, 'pulse', 'range'), may hold values from -6 to 6
- merge_taps: int32 [3, 2, 4, 16384], P(None, None, None, 'pulse'), may hold values from 0 to 1023, as said below
- merge_weights: bfloat16 [3, 2, 4, 16384], P(None, None, None, 'pulse'), may hold values from -2 to 2
- squint: float32 [3, 16384], P(None, 'pulse'), may hold values from -8 to 8
Outputs:
- focused: float32 [2, 1024, 4096], P(None, 'pulse', 'range')
The draws below stay inside these ranges and needn't reach their ends.
Inputs may be any that keep to these rules, and one draw needn't show every extreme that they name: `merge_taps`: for each level, source half and output beam, the 4 taps name different beams of the source block.
All inputs are finite; a program needn't handle non-finite values.
Results may differ from the reference program's by a relative error of at most 0.0064.
Values may be sent and summed in bfloat16 or wider, within the bound.
A program may use at most 64 MiB of HBM per device.

```python
import math
import jax
import jax.numpy as jnp
import numpy as np
from jax import lax

BEAM_DEV = 1024
RANGES = 4096
BINS = 1024
BLOCK = 64
TAPS = 4
LEVELS = 3
POWER = 3
ANGLES = 16384
N_PULSE = 16


def draw_merge_taps(key, part):
    spread = BEAM_DEV // TAPS
    base = jax.random.randint(jax.random.fold_in(key, 11), (LEVELS, 2, 1, ANGLES), 0, BEAM_DEV)
    jitter = jax.random.randint(jax.random.fold_in(key, 12), (LEVELS, 2, TAPS, ANGLES), 0, spread)
    order = lax.broadcasted_iota(jnp.int32, (LEVELS, 2, TAPS, ANGLES), 2)
    offset = jnp.where(order == 0, 0, order * spread + jitter)
    return ((base + offset) % BEAM_DEV).astype(jnp.int32)


def levels(rng, shape, shards, low, largest):
    def one(axis_at, shards_of):
        heights = jax.random.uniform(jax.random.fold_in(jax.random.fold_in(rng, 6), axis_at), (shards_of,), jnp.float32, low / len(shards), largest / len(shards))
        return jnp.repeat(jnp.exp(heights), shape[axis_at] // shards_of).reshape((-1,) + (1,) * (len(shape) - axis_at - 1))

    gain = one(*shards[0])
    for cut in shards[1:]:
        gain = gain * one(*cut)
    return gain


def noise(key, extent, deviation, reach, pieces=(), held_as=jnp.bfloat16):
    loudness = levels(key, extent, pieces, -0.22, 0.18) if pieces else 1.0
    entries = jax.random.normal(key, extent, jnp.float32) * deviation * loudness
    return jnp.minimum(jnp.maximum(entries, -reach), reach).astype(held_as)


def setup_inputs(seed: int = 0) -> dict:
    key_of = jax.random.split(jax.random.key(seed), 5)
    pulse_data = noise(key_of[0], (2, ANGLES, RANGES), 1.0, 6.0, ((1, 16), (2, 16)))
    merge_taps = draw_merge_taps(jax.random.fold_in(key_of[4], 71), 0)
    merge_weights = noise(key_of[2], (LEVELS, 2, TAPS, ANGLES), 0.35, 2.0, ((3, 16),))
    squint = jnp.clip(jax.random.uniform(key_of[3], (LEVELS, ANGLES), jnp.float32, -8.0, 8.0) * levels(key_of[3], (LEVELS, ANGLES), ((1, 16),), -0.4, 0.0), -8.0, 8.0)
    return dict(pulse_data=pulse_data, merge_taps=merge_taps, merge_weights=merge_weights, squint=squint)


TWO_PI = 2.0 * math.pi
EPSILON = 1e-06

def merge_all(pulse_data, merge_taps, merge_weights, squint):
    data = pulse_data.reshape(2, N_PULSE, BEAM_DEV, RANGES).transpose(1, 0, 2, 3)
    range_phase = jnp.arange(RANGES, dtype=jnp.int32).astype(jnp.float32) * (TWO_PI / RANGES)

    def merge_block(items):
        own, other, taps_block, weights_block, squint_block = items
        total = jnp.zeros(own.shape, jnp.float32)
        for source, block in ((0, own), (1, other)):
            for tap in range(TAPS):
                picked = jnp.take(block, taps_block[source, tap], axis=1).astype(jnp.float32)
                total = total + weights_block[source, tap].astype(jnp.float32)[None, :, None] * picked
        phase = squint_block[:, None] * range_phase[None, :]
        cosine = jnp.cos(phase)
        sine = jnp.sin(phase)
        real = cosine * total[0] - sine * total[1]
        imag = sine * total[0] + cosine * total[1]
        return jnp.stack([real, imag]).astype(jnp.bfloat16)
    for level in range(LEVELS):
        partner_order = np.arange(N_PULSE) ^ 1 << level
        other = data[partner_order]
        taps_level = merge_taps[level].reshape(2, TAPS, N_PULSE, BEAM_DEV).transpose(2, 0, 1, 3)
        weights_level = merge_weights[level].reshape(2, TAPS, N_PULSE, BEAM_DEV).transpose(2, 0, 1, 3)
        squint_level = squint[level].reshape(N_PULSE, BEAM_DEV)
        data = lax.map(merge_block, (data, other, taps_level, weights_level, squint_level))
    return data.transpose(1, 0, 2, 3).reshape(2, ANGLES, RANGES)

def reference(pulse_data, merge_taps, merge_weights, squint):
    beams = merge_all(pulse_data, merge_taps, merge_weights, squint).astype(jnp.float32)
    bins_col = jnp.arange(BINS, dtype=jnp.int32)[:, None]
    angle_row = jnp.arange(ANGLES, dtype=jnp.int32)[None, :]
    theta = (bins_col * angle_row % ANGLES).astype(jnp.float32) * (TWO_PI / ANGLES)
    cosine = jnp.cos(theta).astype(jnp.bfloat16).astype(jnp.float32)
    sine = jnp.sin(theta).astype(jnp.bfloat16).astype(jnp.float32)
    along_cos = jnp.einsum('fa,tar->ftr', cosine, beams)
    along_sin = jnp.einsum('fa,tar->ftr', sine, beams)
    scale = ANGLES ** (-0.5)
    spec_re = (along_cos[:, 0] + along_sin[:, 1]) * scale
    spec_im = (along_cos[:, 1] - along_sin[:, 0]) * scale
    blocks = BINS // BLOCK
    g_re = spec_re.reshape(blocks, BLOCK, RANGES)
    g_im = spec_im.reshape(blocks, BLOCK, RANGES)
    highest = lax.Precision.HIGHEST
    cov_re = jnp.einsum('bjr,bkr->bjk', g_re, g_re, precision=highest) + jnp.einsum('bjr,bkr->bjk', g_im, g_im, precision=highest)
    cov_im = jnp.einsum('bjr,bkr->bjk', g_im, g_re, precision=highest) - jnp.einsum('bjr,bkr->bjk', g_re, g_im, precision=highest)
    vec_re = jnp.ones((blocks, BLOCK), jnp.float32)
    vec_im = jnp.zeros((blocks, BLOCK), jnp.float32)
    for step in range(POWER):
        new_re = jnp.einsum('bjk,bk->bj', cov_re, vec_re, precision=highest) - jnp.einsum('bjk,bk->bj', cov_im, vec_im, precision=highest)
        new_im = jnp.einsum('bjk,bk->bj', cov_re, vec_im, precision=highest) + jnp.einsum('bjk,bk->bj', cov_im, vec_re, precision=highest)
        length = jnp.sqrt(lax.optimization_barrier(jnp.sum(new_re * new_re + new_im * new_im, axis=1, keepdims=True)) + EPSILON)
        vec_re = new_re / length
        vec_im = new_im / length
    factor = math.sqrt(BLOCK)
    out_re = (g_re * vec_re[:, :, None] + g_im * vec_im[:, :, None]) * factor
    out_im = (g_im * vec_re[:, :, None] - g_re * vec_im[:, :, None]) * factor
    return jnp.stack([out_re.reshape(BINS, RANGES), out_im.reshape(BINS, RANGES)])
```

```python
import math

import jax
import jax.numpy as jnp
from jax import lax
from jax.experimental import pallas as pl
from jax.experimental.pallas import tpu as pltpu
from jax.sharding import PartitionSpec as P

RANGES = 4096
ANGLES = 16384
BEAMS = 1024
COLS = 256
BLOCK = 64
EPSILON = 1e-06
TWO_PI = 2.0 * math.pi
RANGE_STEP = TWO_PI / RANGES
MESH = pl.DeviceIdType.MESH
f32 = jnp.float32
bf16 = jnp.bfloat16
NT = (((1,), (1,)), ((), ()))


def flipped(index, bit):
    return index + bit - 2 * bit * ((index // bit) % 2)


def kernel(
    data, taps, weights, squint, out,
    dT, prm, snd, W, rowid, rb, rs, S1, U, X, Y, us, tab,
    fst, psn, prx, zsn, zrx, G, F, cx, cy,
    part_s, part_r, prm_s, prm_r, pair_s, pair_r, z_s, z_r, x_s, x_r, y_s, y_r,
):
    pulse = lax.axis_index("pulse")
    ranged = lax.axis_index("range")
    z = pulse // 2
    core = pulse % 2
    gx = ranged // 4
    gy = ranged % 4
    other = 1 - core
    buddy = flipped(pulse, 1)
    q2 = flipped(pulse, 2)
    q4 = flipped(pulse, 4)
    q6 = flipped(q2, 4)

    def z_peer(k):
        return ((z + k) % 8) * 2 + core

    def x_peer(k):
        return ((gx + k) % 4) * 4 + gy

    def y_peer(k):
        return gx * 4 + (gy + k) % 4

    barrier = pltpu.get_barrier_semaphore()
    pl.semaphore_signal(barrier, inc=1, device_id={"pulse": buddy}, device_id_type=MESH)
    for k in range(1, 8):
        pl.semaphore_signal(barrier, inc=1, device_id={"pulse": z_peer(k)}, device_id_type=MESH)
    for k in range(1, 4):
        pl.semaphore_signal(barrier, inc=1, device_id={"range": x_peer(k)}, device_id_type=MESH)
        pl.semaphore_signal(barrier, inc=1, device_id={"range": y_peer(k)}, device_id_type=MESH)

    for t in range(2):
        dT[0, t * COLS:(t + 1) * COLS, :] = data[t].T

    def fill(ref, level, source):
        ref[0:4, :] = taps[level, source].astype(f32)
        ref[4:8, :] = weights[level, source].astype(f32)
        ref[8:9, :] = squint[level:level + 1, :]

    fill(snd.at[0], 1, 1)
    fill(snd.at[1], 2, 1)
    fill(prm.at[4], 2, 0)

    pl.semaphore_wait(barrier, 14)

    part = pltpu.make_async_remote_copy(
        dT.at[0], dT.at[1], part_s, part_r, device_id={"pulse": buddy}, device_id_type=MESH)
    part.start()
    prm_copies = []
    for n, (src, slot, target) in enumerate((
        (snd.at[1], 7, q6), (snd.at[1], 5, q4), (snd.at[0], 3, q2), (prm.at[4], 6, q2))):
        copy = pltpu.make_async_remote_copy(
            src, prm.at[slot], prm_s.at[n], prm_r.at[n],
            device_id={"pulse": target}, device_id_type=MESH)
        copy.start()
        prm_copies.append(copy)

    fill(prm.at[0], 0, 0)
    fill(prm.at[1], 0, 1)
    fill(prm.at[2], 1, 0)

    rowid[...] = lax.broadcasted_iota(jnp.int32, (256, 256), 0).astype(f32).astype(bf16)

    def build(m):
        def tile(step, carry):
            nt = step // 4
            kb = step % 4
            cols = pl.ds(pl.multiple_of(nt * 256, 256), 256)
            base = (kb * 256).astype(f32)
            rows = rowid[...]
            val = jnp.zeros((256, 256), bf16)
            for tap in range(4):
                place = (prm[m, tap:tap + 1, cols] - base).astype(bf16)
                weight = prm[m, 4 + tap:5 + tap, cols].astype(bf16)
                val = jnp.where(rows == place, weight, val)
            W[m, nt, pl.ds(pl.multiple_of(kb * 256, 256), 256), :] = val
            return carry

        lax.fori_loop(0, 16, tile, 0)

    first_range = (ranged * COLS).astype(f32)

    def prepare_rotation(m):
        slope = prm[m, 8:9, :]
        i8 = lax.broadcasted_iota(jnp.int32, (8, BEAMS), 0).astype(f32)
        phase = slope * ((i8 + first_range) * RANGE_STEP)
        c0 = jnp.cos(phase)
        s0 = jnp.sin(phase)
        far = slope * (jnp.where(i8 < 1.0, 8.0, 128.0) * RANGE_STEP)
        cf = jnp.cos(far)
        sf = jnp.sin(far)
        rb[m, 0, 0] = c0
        rb[m, 0, 1] = s0
        ch = cf[1:2]
        sh = sf[1:2]
        rb[m, 1, 0] = c0 * ch - s0 * sh
        rb[m, 1, 1] = s0 * ch + c0 * sh
        rs[m, 0] = jnp.broadcast_to(cf[0:1], (8, BEAMS))
        rs[m, 1] = jnp.broadcast_to(sf[0:1], (8, BEAMS))

    def rotated(real, imag, m, half, cols):
        c = rb[m, half, 0, :, cols]
        s = rb[m, half, 1, :, cols]
        c8 = rs[m, 0, :, cols]
        s8 = rs[m, 1, :, cols]
        reals = []
        imags = []
        for i in range(real.shape[0] // 8):
            a = real[8 * i:8 * i + 8]
            b = imag[8 * i:8 * i + 8]
            reals.append(c * a - s * b)
            imags.append(s * a + c * b)
            c, s = c * c8 - s * s8, s * c8 + c * s8
        return jnp.concatenate(reals, axis=0), jnp.concatenate(imags, axis=0)

    for m in (0, 1, 2, 4):
        build(m)
        if m != 1:
            prepare_rotation(m)

    part.wait()

    def level0(nt, carry):
        cols = pl.ds(pl.multiple_of(nt * 256, 256), 256)
        acc = jnp.dot(dT[0], W[0, nt], preferred_element_type=f32)
        acc = acc + jnp.dot(dT[1], W[1, nt], preferred_element_type=f32)
        for half in range(2):
            re, im = rotated(
                acc[128 * half:128 * half + 128],
                acc[256 + 128 * half:256 + 128 * half + 128], 0, half, cols)
            S1[half, 0:128, cols] = re.astype(bf16)
            S1[half, 128:256, cols] = im.astype(bf16)
        return carry

    lax.fori_loop(0, 4, level0, 0)

    for copy in prm_copies:
        copy.wait()

    for m in (3, 5, 6, 7):
        build(m)
        prepare_rotation(m)

    angle = lax.broadcasted_iota(jnp.int32, (16, BEAMS), 1) + BEAMS * (core + 8 * (z // 4))
    up = lax.broadcasted_iota(jnp.int32, (16, BEAMS), 0)
    theta = ((64 * up * angle) % ANGLES).astype(f32) * (TWO_PI / ANGLES)
    us[0] = jnp.cos(theta)
    us[1] = jnp.sin(theta)

    def table(k, carry):
        a8 = lax.broadcasted_iota(jnp.int32, (8, BEAMS), 1) + BEAMS * (core + 8 * (z // 4))
        v8 = 8 * lax.broadcasted_iota(jnp.int32, (8, BEAMS), 0) + k
        small = ((v8 * a8) % ANGLES).astype(f32) * (TWO_PI / ANGLES)
        vc = jnp.cos(small)
        vs = jnp.sin(small)
        for pair in range(8):
            cs = []
            ss = []
            for u in (2 * pair, 2 * pair + 1):
                uc = us[0, u:u + 1, :]
                un = us[1, u:u + 1, :]
                cs.append(uc * vc - un * vs)
                ss.append(un * vc + uc * vs)
            tab[k, 16 * pair:16 * pair + 16, :] = jnp.concatenate(cs, axis=0).astype(bf16)
            tab[k, 128 + 16 * pair:144 + 16 * pair, :] = jnp.concatenate(ss, axis=0).astype(bf16)
        return carry

    lax.fori_loop(0, 8, table, 0)

    root = math.sqrt(0.5)

    def level1(half):
        def body(nt, carry):
            cols = pl.ds(pl.multiple_of(nt * 256, 256), 256)
            for j in range(2):
                acc = jnp.dot(S1[half], W[2 + j, nt], preferred_element_type=f32)
                re, im = rotated(acc[:128], acc[128:], 2 + j, half, cols)
                U[j, 0:128, cols] = re.astype(bf16)
                U[j, 128:256, cols] = im.astype(bf16)
            return carry

        lax.fori_loop(0, 4, body, 0)

    bit0 = z % 2
    bit1 = (z // 2) % 2

    def level2(half):
        def body(nt, carry):
            cols = pl.ds(pl.multiple_of(nt * 256, 256), 256)
            for i, m in enumerate((4, 6, 5, 7)):
                acc = jnp.dot(U[i % 2], W[m, nt], preferred_element_type=f32)
                re, im = rotated(acc[:128], acc[128:], m, half, cols)
                at0 = bit0 if i % 2 == 0 else 1 - bit0
                at1 = bit1 if i // 2 == 0 else 1 - bit1
                slot = at0 + 2 * at1
                X[slot, 0:128, :] = re
                X[slot, 128:256, :] = im

            def rows16(step, carry):
                top = pl.ds(pl.multiple_of(step * 16, 16), 16)
                low = pl.ds(pl.multiple_of(128 + step * 16, 16), 16)
                xr = [X[n, top, :] for n in range(4)]
                xi = [X[n, low, :] for n in range(4)]
                e = [
                    (xr[0] + xr[2], xi[0] + xi[2]),
                    (xr[0] + xi[2], xi[0] - xr[2]),
                    (xr[0] - xr[2], xi[0] - xi[2]),
                    (xr[0] - xi[2], xi[0] + xr[2]),
                ]
                o = [
                    (xr[1] + xr[3], xi[1] + xi[3]),
                    (xr[1] + xi[3], xi[1] - xr[3]),
                    (xr[1] - xr[3], xi[1] - xi[3]),
                    (xr[1] - xi[3], xi[1] + xr[3]),
                ]
                t = [
                    o[0],
                    (root * (o[1][0] + o[1][1]), root * (o[1][1] - o[1][0])),
                    (o[2][1], -o[2][0]),
                    (root * (o[3][1] - o[3][0]), -root * (o[3][0] + o[3][1])),
                ]
                for k in range(4):
                    Y[k, top, cols] = (e[k][0] + t[k][0]).astype(bf16)
                    Y[k, low, cols] = (e[k][1] + t[k][1]).astype(bf16)
                    Y[k + 4, top, cols] = (e[k][0] - t[k][0]).astype(bf16)
                    Y[k + 4, low, cols] = (e[k][1] - t[k][1]).astype(bf16)
                return carry

            lax.fori_loop(0, 8, rows16, 0)
            return carry

        lax.fori_loop(0, 4, body, 0)

    scale = ANGLES ** (-0.5)

    def spectrum(half):
        def body(kk, carry):
            res = []
            ims = []
            for e in range(2):
                both = lax.dot_general(
                    tab[2 * kk + e], Y[2 * kk + e], NT, preferred_element_type=f32)
                res.append((both[:128, :128] + both[128:, 128:]) * scale)
                ims.append((both[:128, 128:] - both[128:, :128]) * scale)
            for t, parts in enumerate((res, ims)):
                val = jnp.concatenate([p.reshape(16, 8, 128) for p in parts], axis=1)
                val = val.reshape(8, 2, 16, 128)
                for c in range(2):
                    fst[half, c, :, kk, t] = val[:, c]
            return carry

        lax.fori_loop(0, 4, body, 0)

        def narrow(d, carry):
            psn[half, d] = fst[half, other, d].astype(bf16)
            return carry

        lax.fori_loop(0, 8, narrow, 0)

    def pair_copy(half):
        return pltpu.make_async_remote_copy(
            psn.at[half], prx.at[half], pair_s.at[half], pair_r.at[half],
            device_id={"pulse": buddy}, device_id_type=MESH)

    order = (4, 3, 5, 2, 6, 1, 7)

    def z_copy(half, k):
        return pltpu.make_async_remote_copy(
            zsn.at[half, (z + k) % 8], zrx.at[half, k - 1],
            z_s.at[half, k - 1], z_r.at[half, k - 1],
            device_id={"pulse": z_peer(k)}, device_id_type=MESH)

    def scatter(half):
        pair_copy(half).wait()

        def add(d, carry):
            zsn[half, d] = (fst[half, core, d] + prx[half, d].astype(f32)).astype(bf16)
            return carry

        lax.fori_loop(0, 8, add, 0)
        for k in order:
            z_copy(half, k).start()

    level1(0)
    level2(0)
    spectrum(0)
    pair_copy(0).start()
    level1(1)
    scatter(0)
    level2(1)
    spectrum(1)
    pair_copy(1).start()
    scatter(1)

    for half in range(2):
        total = fst[half, core, z] + prx[half, z].astype(f32)
        for k in order:
            z_copy(half, k).wait()
            total = total + zrx[half, k - 1].astype(f32)
        for kk in range(4):
            for t in range(2):
                G[64 * t + 16 * kk:64 * t + 16 * kk + 16, 128 * half:128 * half + 128] = total[kk, t]

    gg = G[...]
    m = lax.dot_general(gg, gg, NT, precision=lax.Precision.HIGHEST, preferred_element_type=f32)
    lane = lax.broadcasted_iota(jnp.int32, (64, 128), 1)
    sign = jnp.where(lane < 64, 1.0, -1.0).astype(f32)
    cov = m[:64] * sign + pltpu.roll(m[64:], 64, 1)

    def reduced(mine, here, buf, send, recv, axis_peer):
        buf[here] = mine
        copies = []
        for k in (2, 1, 3):
            copy = pltpu.make_async_remote_copy(
                buf.at[here], buf.at[here], send.at[k - 1], recv.at[k - 1],
                device_id={"range": axis_peer(k)}, device_id_type=MESH)
            copy.start()
            copies.append(copy)
        for copy in copies:
            copy.wait()
        return (buf[0] + buf[1]) + (buf[2] + buf[3])

    cov = reduced(cov, gx, cx, x_s, x_r, x_peer)
    cov = reduced(cov, gy, cy, y_s, y_r, y_peer)

    K = jnp.concatenate([cov * sign, pltpu.roll(cov, 64, 1)], axis=0)
    wide = lax.broadcasted_iota(jnp.int32, (128, 128), 1)
    w = jnp.sum(jnp.where(wide < 64, K, 0.0), axis=1, keepdims=True)
    v = w / jnp.sqrt(jnp.sum(w * w, axis=0, keepdims=True) + EPSILON)
    w = jnp.sum(K * v, axis=0, keepdims=True)
    v = w / jnp.sqrt(jnp.sum(w * w, axis=1, keepdims=True) + EPSILON)
    w = jnp.sum(K * v, axis=1, keepdims=True)
    v = w / jnp.sqrt(jnp.sum(w * w, axis=0, keepdims=True) + EPSILON)
    v = v * math.sqrt(BLOCK)
    vr = v[:64]
    vi = v[64:]
    gr = gg[:64]
    gi = gg[64:]
    focused = (gr * vr + gi * vi, gi * vr - gr * vi)
    for t in range(2):
        for k in range(8):
            for half in range(2):
                F[t, half, pl.ds(k, 8, stride=8), :] = focused[t][8 * k:8 * k + 8, 128 * half:128 * half + 128]
        for half in range(2):
            out[t, :, 128 * half:128 * half + 128] = F[t, half]


def per_device(pulse_data, merge_taps, merge_weights, squint):
    vmem = pl.BlockSpec(memory_space=pltpu.VMEM)
    dma = pltpu.SemaphoreType.DMA
    return pl.pallas_call(
        kernel,
        out_shape=jax.ShapeDtypeStruct((2, BLOCK, COLS), f32),
        in_specs=[vmem] * 4,
        out_specs=vmem,
        scratch_shapes=[
            pltpu.VMEM((2, 512, BEAMS), bf16),
            pltpu.VMEM((8, 16, BEAMS), f32),
            pltpu.VMEM((2, 16, BEAMS), f32),
            pltpu.VMEM((8, 4, BEAMS, 256), bf16),
            pltpu.VMEM((256, 256), bf16),
            pltpu.VMEM((8, 2, 2, 8, BEAMS), f32),
            pltpu.VMEM((8, 2, 8, BEAMS), f32),
            pltpu.VMEM((2, 256, BEAMS), bf16),
            pltpu.VMEM((2, 256, BEAMS), bf16),
            pltpu.VMEM((4, 256, 256), f32),
            pltpu.VMEM((8, 256, BEAMS), bf16),
            pltpu.VMEM((2, 16, BEAMS), f32),
            pltpu.VMEM((8, 256, BEAMS), bf16),
            pltpu.VMEM((2, 2, 8, 4, 2, 16, 128), f32),
            pltpu.VMEM((2, 8, 4, 2, 16, 128), bf16),
            pltpu.VMEM((2, 8, 4, 2, 16, 128), bf16),
            pltpu.VMEM((2, 8, 4, 2, 16, 128), bf16),
            pltpu.VMEM((2, 7, 4, 2, 16, 128), bf16),
            pltpu.VMEM((128, COLS), f32),
            pltpu.VMEM((2, 2, 64, 128), f32),
            pltpu.VMEM((4, 64, 128), f32),
            pltpu.VMEM((4, 64, 128), f32),
            dma, dma,
            dma((4,)), dma((4,)),
            dma((2,)), dma((2,)),
            dma((2, 7)), dma((2, 7)),
            dma((3,)), dma((3,)),
            dma((3,)), dma((3,)),
        ],
        compiler_params=pltpu.CompilerParams(
            collective_id=0, has_side_effects=True, vmem_limit_bytes=60 * 1024 * 1024),
    )(pulse_data, merge_taps, merge_weights, squint)


def solution(mesh):
    placed = (
        P(None, "pulse", "range"),
        P(None, None, None, "pulse"),
        P(None, None, None, "pulse"),
        P(None, "pulse"),
    )
    return jax.shard_map(
        per_device, mesh=mesh, in_specs=placed, out_specs=P(None, "pulse", "range"), check_vma=False
    )
```

```python
import math

import jax
import jax.numpy as jnp
from jax import lax
from jax.experimental import pallas as pl
from jax.experimental.pallas import tpu as pltpu
from jax.sharding import PartitionSpec as P

RANGES = 4096
ANGLES = 16384
BEAMS = 1024
COLS = 256
BLOCK = 64
EPSILON = 1e-06
TWO_PI = 2.0 * math.pi
COS_TERMS = [(-1) ** k * TWO_PI ** (2 * k) / math.factorial(2 * k) for k in range(10)]
SIN_TERMS = [(-1) ** k * TWO_PI ** (2 * k + 1) / math.factorial(2 * k + 1) for k in range(9)]
MESH = pl.DeviceIdType.MESH
f32 = jnp.float32
bf16 = jnp.bfloat16
NT = (((1,), (1,)), ((), ()))


def flipped(index, bit):
    return index + bit - 2 * bit * ((index // bit) % 2)


def sincos(turns):
    part = turns - jnp.floor(turns + 0.5)
    y = part * part
    c = jnp.full_like(y, COS_TERMS[-1])
    for term in COS_TERMS[-2::-1]:
        c = c * y + term
    s = jnp.full_like(y, SIN_TERMS[-1])
    for term in SIN_TERMS[-2::-1]:
        s = s * y + term
    return c, s * part


def kernel(
    data_hbm, taps, weights, squint, out,
    data, dT, prm, snd, W, rowid, rb, rs, acc, S1, U, X, Y, us, tab,
    fst, stg, prx, zsn, zrx, G, F, cx,
    load_s, part_s, part_r, prm_s, prm_r, pair_s, pair_r, z_s, z_r, c_s, c_r,
):
    pulse = lax.axis_index("pulse")
    ranged = lax.axis_index("range")
    z = pulse // 2
    core = pulse % 2
    gx = ranged // 4
    gy = ranged % 4
    other = 1 - core
    buddy = flipped(pulse, 1)
    q2 = flipped(pulse, 2)
    q4 = flipped(pulse, 4)
    q6 = flipped(q2, 4)

    def z_peer(k):
        return ((z + k) % 8) * 2 + core

    def r_peer(k):
        return ((gx + k // 4) % 4) * 4 + (gy + k % 4) % 4

    load = pltpu.make_async_copy(data_hbm, data, load_s)
    load.start()

    barrier = pltpu.get_barrier_semaphore()
    pl.semaphore_signal(barrier, inc=1, device_id={"pulse": buddy}, device_id_type=MESH)
    for k in range(1, 8):
        pl.semaphore_signal(barrier, inc=1, device_id={"pulse": z_peer(k)}, device_id_type=MESH)
    for k in range(1, 16):
        pl.semaphore_signal(barrier, inc=1, device_id={"range": r_peer(k)}, device_id_type=MESH)

    def fill(ref, level, source):
        ref[0:4, :] = taps[level, source].astype(f32)
        ref[4:8, :] = weights[level, source].astype(f32)
        ref[8:9, :] = squint[level:level + 1, :]

    fill(snd.at[0], 1, 1)
    fill(snd.at[1], 2, 1)
    fill(prm.at[4], 2, 0)
    fill(prm.at[0], 0, 0)
    fill(prm.at[1], 0, 1)
    fill(prm.at[2], 1, 0)
    rowid[...] = lax.broadcasted_iota(jnp.int32, (256, 256), 0).astype(f32).astype(bf16)

    def build(m, slot):
        for nt in range(4):
            cols = slice(256 * nt, 256 * nt + 256)
            places = [prm[m, tap:tap + 1, cols] for tap in range(4)]
            scales = [prm[m, 4 + tap:5 + tap, cols].astype(bf16) for tap in range(4)]
            for kb in range(4):
                val = jnp.zeros((256, 256), bf16)
                for tap in range(4):
                    here = rowid[...] == (places[tap] - 256.0 * kb).astype(bf16)
                    val = jnp.where(here, scales[tap], val)
                W[slot, 256 * kb:256 * kb + 256, cols] = val

    first_range = (ranged * COLS).astype(f32)

    def prepare_rotation(m):
        slope = prm[m, 8:9, :]
        i8 = lax.broadcasted_iota(jnp.int32, (8, BEAMS), 0).astype(f32)
        c0, s0 = sincos(slope * ((i8 + first_range) * (1.0 / RANGES)))
        cf, sf = sincos(slope * (jnp.where(i8 < 1.0, 8.0, 128.0) * (1.0 / RANGES)))
        rb[m, 0, 0] = c0
        rb[m, 0, 1] = s0
        ch = cf[1:2]
        sh = sf[1:2]
        rb[m, 1, 0] = c0 * ch - s0 * sh
        rb[m, 1, 1] = s0 * ch + c0 * sh
        rs[m, 0] = jnp.broadcast_to(cf[0:1], (8, BEAMS))
        rs[m, 1] = jnp.broadcast_to(sf[0:1], (8, BEAMS))

    def rotate(src, m, half, dest, kind, re_at, im_at):
        for nt in range(4):
            cols = slice(256 * nt, 256 * nt + 256)
            c = rb[m, half, 0, :, cols]
            s = rb[m, half, 1, :, cols]
            c8 = rs[m, 0, :, cols]
            s8 = rs[m, 1, :, cols]
            for i in range(8):
                reals = []
                imags = []
                for e in range(2):
                    q = 16 * i + 8 * e
                    a = src[re_at + q:re_at + q + 8, cols]
                    b = src[im_at + q:im_at + q + 8, cols]
                    reals.append(c * a - s * b)
                    imags.append(s * a + c * b)
                    c, s = c * c8 - s * s8, s * c8 + c * s8
                q = 128 * half + 16 * i
                dest[q:q + 16, cols] = jnp.concatenate(reals, axis=0).astype(kind)
                dest[256 + q:272 + q, cols] = jnp.concatenate(imags, axis=0).astype(kind)

    def rotate_all(src, m, dest, kind):
        for half in range(2):
            rotate(src, m, half, dest, kind, 128 * half, 256 + 128 * half)

    first_angle = BEAMS * (core + 8 * (z // 4))

    def table_base():
        angle = lax.broadcasted_iota(jnp.int32, (16, BEAMS), 1) + first_angle
        up = lax.broadcasted_iota(jnp.int32, (16, BEAMS), 0)
        us[0], us[1] = sincos(((64 * up * angle) % ANGLES).astype(f32) * (1.0 / ANGLES))

    def table(k):
        a8 = lax.broadcasted_iota(jnp.int32, (8, BEAMS), 1) + first_angle
        v8 = 8 * lax.broadcasted_iota(jnp.int32, (8, BEAMS), 0) + k
        vc, vs = sincos(((v8 * a8) % ANGLES).astype(f32) * (1.0 / ANGLES))
        for pair in range(8):
            cs = []
            ss = []
            for u in (2 * pair, 2 * pair + 1):
                uc = us[0, u:u + 1, :]
                un = us[1, u:u + 1, :]
                cs.append(uc * vc - un * vs)
                ss.append(un * vc + uc * vs)
            tab[k, 16 * pair:16 * pair + 16, :] = jnp.concatenate(cs, axis=0).astype(bf16)
            tab[k, 128 + 16 * pair:144 + 16 * pair, :] = jnp.concatenate(ss, axis=0).astype(bf16)

    build(0, 0)
    prepare_rotation(0)
    table_base()

    load.wait()
    for t in range(2):
        dT[0, t * COLS:(t + 1) * COLS, :] = data[t].T

    pl.semaphore_wait(barrier, 23)

    part = pltpu.make_async_remote_copy(
        dT.at[0], dT.at[1], part_s, part_r, device_id={"pulse": buddy}, device_id_type=MESH)
    part.start()
    prm_copies = []
    for n, (src, slot, target) in enumerate((
        (snd.at[1], 7, q6), (snd.at[1], 5, q4), (snd.at[0], 3, q2), (prm.at[4], 6, q2))):
        copy = pltpu.make_async_remote_copy(
            src, prm.at[slot], prm_s.at[n], prm_r.at[n],
            device_id={"pulse": target}, device_id_type=MESH)
        copy.start()
        prm_copies.append(copy)

    acc[0] = jnp.dot(dT[0], W[0], preferred_element_type=f32)
    build(1, 1)
    prepare_rotation(2)
    table(0)
    part.wait()
    acc[1] = jnp.dot(dT[1], W[1], preferred_element_type=f32) + acc[0]
    build(2, 0)
    table(1)
    for copy in prm_copies:
        copy.wait()
    rotate_all(acc.at[1], 0, S1, bf16)

    acc[0] = jnp.dot(S1[...], W[0], preferred_element_type=f32)
    build(3, 1)
    prepare_rotation(3)
    table(2)

    acc[1] = jnp.dot(S1[...], W[1], preferred_element_type=f32)
    build(4, 0)
    rotate_all(acc.at[0], 2, U.at[0], bf16)
    prepare_rotation(4)
    table(3)

    bit0 = z % 2
    bit1 = (z // 2) % 2

    def slot_of(i):
        at0 = bit0 if i % 2 == 0 else 1 - bit0
        at1 = bit1 if i // 2 == 0 else 1 - bit1
        return at0 + 2 * at1

    acc[0] = jnp.dot(U[0], W[0], preferred_element_type=f32)
    build(5, 1)
    rotate_all(acc.at[1], 3, U.at[1], bf16)
    prepare_rotation(5)
    table(4)

    acc[1] = jnp.dot(U[0], W[1], preferred_element_type=f32)
    build(6, 0)
    rotate_all(acc.at[0], 4, X.at[slot_of(0)], f32)
    prepare_rotation(6)
    table(5)

    acc[0] = jnp.dot(U[1], W[0], preferred_element_type=f32)
    build(7, 1)
    rotate_all(acc.at[1], 5, X.at[slot_of(2)], f32)
    prepare_rotation(7)
    table(6)

    def last(half):
        lhs = jnp.concatenate(
            [U[1, 128 * half:128 * half + 128, :], U[1, 256 + 128 * half:384 + 128 * half, :]], axis=0)
        acc[1, 256 * half:256 * half + 256, :] = jnp.dot(lhs, W[1], preferred_element_type=f32)

    root = math.sqrt(0.5)

    def combine(half, nt):
        cols = pl.ds(nt * 256, 256) if isinstance(nt, int) else pl.ds(pl.multiple_of(nt * 256, 256), 256)
        for step in range(8):
            top = slice(128 * half + 16 * step, 128 * half + 16 * step + 16)
            low = slice(256 + 128 * half + 16 * step, 272 + 128 * half + 16 * step)
            xr = [X[n, top, cols] for n in range(4)]
            xi = [X[n, low, cols] for n in range(4)]
            e = [
                (xr[0] + xr[2], xi[0] + xi[2]),
                (xr[0] + xi[2], xi[0] - xr[2]),
                (xr[0] - xr[2], xi[0] - xi[2]),
                (xr[0] - xi[2], xi[0] + xr[2]),
            ]
            o = [
                (xr[1] + xr[3], xi[1] + xi[3]),
                (xr[1] + xi[3], xi[1] - xr[3]),
                (xr[1] - xr[3], xi[1] - xi[3]),
                (xr[1] - xi[3], xi[1] + xr[3]),
            ]
            t = [
                o[0],
                (root * (o[1][0] + o[1][1]), root * (o[1][1] - o[1][0])),
                (o[2][1], -o[2][0]),
                (root * (o[3][1] - o[3][0]), -root * (o[3][0] + o[3][1])),
            ]
            top = slice(16 * step, 16 * step + 16)
            low = slice(128 + 16 * step, 144 + 16 * step)
            for k in range(4):
                Y[half, k, top, cols] = (e[k][0] + t[k][0]).astype(bf16)
                Y[half, k, low, cols] = (e[k][1] + t[k][1]).astype(bf16)
                Y[half, k + 4, top, cols] = (e[k][0] - t[k][0]).astype(bf16)
                Y[half, k + 4, low, cols] = (e[k][1] - t[k][1]).astype(bf16)

    scale = ANGLES ** (-0.5)

    def spectrum(half, beside):
        def body(kk, carry):
            res = []
            ims = []
            for e in range(2):
                both = lax.dot_general(
                    tab[2 * kk + e], Y[half, 2 * kk + e], NT, preferred_element_type=f32)
                res.append((both[:128, :128] + both[128:, 128:]) * scale)
                ims.append((both[:128, 128:] - both[128:, :128]) * scale)
            for t, parts in enumerate((res, ims)):
                val = jnp.concatenate([p.reshape(16, 8, 128) for p in parts], axis=1)
                val = val.reshape(8, 2, 16, 128)
                for c in range(2):
                    fst[half, c, :, kk, t] = val[:, c]
                    stg[half, c, :, kk, t] = val[:, c].astype(bf16)
            if beside is not None:
                combine(beside, kk)
            return carry

        lax.fori_loop(0, 4, body, 0)

    def pair_copy(half):
        return pltpu.make_async_remote_copy(
            stg.at[half, other], prx.at[half], pair_s.at[half], pair_r.at[half],
            device_id={"pulse": buddy}, device_id_type=MESH)

    order = (4, 3, 5, 2, 6, 1, 7)

    def z_copy(half, k):
        return pltpu.make_async_remote_copy(
            zsn.at[half, (z + k) % 8], zrx.at[half, k - 1],
            z_s.at[half, k - 1], z_r.at[half, k - 1],
            device_id={"pulse": z_peer(k)}, device_id_type=MESH)

    def scatter(half):
        pair_copy(half).wait()
        for d in range(8):
            zsn[half, d] = (fst[half, core, d] + prx[half, d].astype(f32)).astype(bf16)
        for k in order:
            z_copy(half, k).start()

    last(0)
    rotate_all(acc.at[0], 6, X.at[slot_of(1)], f32)
    table(7)
    rotate(acc.at[1], 7, 0, X.at[slot_of(3)], f32, 0, 128)
    last(1)
    for nt in range(4):
        combine(0, nt)
    rotate(acc.at[1], 7, 1, X.at[slot_of(3)], f32, 256, 384)
    spectrum(0, 1)
    pair_copy(0).start()
    scatter(0)
    spectrum(1, None)
    pair_copy(1).start()
    scatter(1)

    for half in range(2):
        total = fst[half, core, z] + prx[half, z].astype(f32)
        for k in order:
            z_copy(half, k).wait()
            total = total + zrx[half, k - 1].astype(f32)
        for kk in range(4):
            for t in range(2):
                G[64 * t + 16 * kk:64 * t + 16 * kk + 16, 128 * half:128 * half + 128] = total[kk, t]

    gg = G[...]
    m = lax.dot_general(gg, gg, NT, precision=lax.Precision.HIGHEST, preferred_element_type=f32)
    lane = lax.broadcasted_iota(jnp.int32, (64, 128), 1)
    row = lax.broadcasted_iota(jnp.int32, (64, 128), 0)
    sign = jnp.where(lane < 64, 1.0, -1.0).astype(f32)
    cov = m[:64] * sign + pltpu.roll(m[64:], 64, 1)
    packed = jnp.where(lane <= row, cov, pltpu.roll(cov, 64, 1))
    packed = jnp.where(lane[:32] < 64, packed[:32], pltpu.roll(packed[32:], 64, 1))

    cx[ranged] = packed
    copies = []
    for k in (10, 9, 11, 6, 14, 2, 8, 5, 7, 13, 15, 1, 3, 4, 12):
        copy = pltpu.make_async_remote_copy(
            cx.at[ranged], cx.at[ranged], c_s.at[k - 1], c_r.at[k - 1],
            device_id={"range": r_peer(k)}, device_id_type=MESH)
        copy.start()
        copies.append(copy)
    for copy in copies:
        copy.wait()
    sums = [cx[n] for n in range(16)]
    while len(sums) > 1:
        sums = [sums[n] + sums[n + 1] for n in range(0, len(sums), 2)]
    packed = jnp.concatenate([sums[0], pltpu.roll(sums[0], 64, 1)], axis=0)
    square = jnp.concatenate([packed, packed], axis=0)
    flip = square.T[:64]
    c_re = jnp.where(lane <= row, packed, flip)
    c_im = jnp.where(lane > row, packed, jnp.where(lane < row, -flip, 0.0))

    K = jnp.concatenate([
        jnp.where(lane < 64, c_re, -pltpu.roll(c_im, 64, 1)),
        jnp.where(lane < 64, c_im, pltpu.roll(c_re, 64, 1)),
    ], axis=0)
    wide = lax.broadcasted_iota(jnp.int32, (128, 128), 1)
    w = jnp.sum(jnp.where(wide < 64, K, 0.0), axis=1, keepdims=True)
    v = w / jnp.sqrt(jnp.sum(w * w, axis=0, keepdims=True) + EPSILON)
    w = jnp.sum(K * v, axis=0, keepdims=True)
    v = w / jnp.sqrt(jnp.sum(w * w, axis=1, keepdims=True) + EPSILON)
    w = jnp.sum(K * v, axis=1, keepdims=True)
    v = w / jnp.sqrt(jnp.sum(w * w, axis=0, keepdims=True) + EPSILON)
    v = v * math.sqrt(BLOCK)
    vr = v[:64]
    vi = v[64:]
    gr = gg[:64]
    gi = gg[64:]
    focused = (gr * vr + gi * vi, gi * vr - gr * vi)
    for t in range(2):
        for k in range(8):
            for half in range(2):
                F[t, half, pl.ds(k, 8, stride=8), :] = focused[t][8 * k:8 * k + 8, 128 * half:128 * half + 128]
        for half in range(2):
            out[t, :, 128 * half:128 * half + 128] = F[t, half]


def per_device(pulse_data, merge_taps, merge_weights, squint):
    vmem = pl.BlockSpec(memory_space=pltpu.VMEM)
    dma = pltpu.SemaphoreType.DMA
    return pl.pallas_call(
        kernel,
        out_shape=jax.ShapeDtypeStruct((2, BLOCK, COLS), f32),
        in_specs=[pl.BlockSpec(memory_space=pl.ANY)] + [vmem] * 3,
        out_specs=vmem,
        scratch_shapes=[
            pltpu.VMEM((2, BEAMS, COLS), bf16),
            pltpu.VMEM((2, 512, BEAMS), bf16),
            pltpu.VMEM((8, 16, BEAMS), f32),
            pltpu.VMEM((2, 16, BEAMS), f32),
            pltpu.VMEM((2, BEAMS, BEAMS), bf16),
            pltpu.VMEM((256, 256), bf16),
            pltpu.VMEM((8, 2, 2, 8, BEAMS), f32),
            pltpu.VMEM((8, 2, 8, BEAMS), f32),
            pltpu.VMEM((2, 512, BEAMS), f32),
            pltpu.VMEM((512, BEAMS), bf16),
            pltpu.VMEM((2, 512, BEAMS), bf16),
            pltpu.VMEM((4, 512, BEAMS), f32),
            pltpu.VMEM((2, 8, 256, BEAMS), bf16),
            pltpu.VMEM((2, 16, BEAMS), f32),
            pltpu.VMEM((8, 256, BEAMS), bf16),
            pltpu.VMEM((2, 2, 8, 4, 2, 16, 128), f32),
            pltpu.VMEM((2, 2, 8, 4, 2, 16, 128), bf16),
            pltpu.VMEM((2, 8, 4, 2, 16, 128), bf16),
            pltpu.VMEM((2, 8, 4, 2, 16, 128), bf16),
            pltpu.VMEM((2, 7, 4, 2, 16, 128), bf16),
            pltpu.VMEM((128, COLS), f32),
            pltpu.VMEM((2, 2, 64, 128), f32),
            pltpu.VMEM((16, 32, 128), f32),
            dma, dma, dma,
            dma((4,)), dma((4,)),
            dma((2,)), dma((2,)),
            dma((2, 7)), dma((2, 7)),
            dma((15,)), dma((15,)),
        ],
        compiler_params=pltpu.CompilerParams(
            collective_id=0, has_side_effects=True, vmem_limit_bytes=60 * 1024 * 1024),
    )(pulse_data, merge_taps, merge_weights, squint)


def solution(mesh):
    placed = (
        P(None, "pulse", "range"),
        P(None, None, None, "pulse"),
        P(None, None, None, "pulse"),
        P(None, "pulse"),
    )
    return jax.shard_map(
        per_device, mesh=mesh, in_specs=placed, out_specs=P(None, "pulse", "range"), check_vma=False
    )
```

```python
import math

import jax
import jax.numpy as jnp
from jax import lax
from jax.experimental import pallas as pl
from jax.experimental.pallas import tpu as pltpu
from jax.sharding import PartitionSpec as P

RANGES = 4096
ANGLES = 16384
BEAMS = 1024
COLS = 256
BLOCK = 64
EPSILON = 1e-06
TWO_PI = 2.0 * math.pi
COS_TERMS = [(-1) ** k * TWO_PI ** (2 * k) / math.factorial(2 * k) for k in range(10)]
SIN_TERMS = [(-1) ** k * TWO_PI ** (2 * k + 1) / math.factorial(2 * k + 1) for k in range(9)]
MESH = pl.DeviceIdType.MESH
f32 = jnp.float32
bf16 = jnp.bfloat16
NT = (((1,), (1,)), ((), ()))


def flipped(index, bit):
    return index + bit - 2 * bit * ((index // bit) % 2)


def sincos(turns):
    part = turns - jnp.floor(turns + 0.5)
    y = part * part
    c = jnp.full_like(y, COS_TERMS[-1])
    for term in COS_TERMS[-2::-1]:
        c = c * y + term
    s = jnp.full_like(y, SIN_TERMS[-1])
    for term in SIN_TERMS[-2::-1]:
        s = s * y + term
    return c, s * part


def kernel(
    data_hbm, taps, weights, squint, out,
    data, dT, prm, snd, W, rowid, rb, rs, acc, S1, U, X, Y, us, tab,
    fst, stg, prx, zsn, near, far, cmb, zrx, G, F, cx,
    load_s, part_s, part_r, prm_s, prm_r, pair_s, pair_r,
    near_s, near_r, far_s, far_r, z_s, z_r, c_s, c_r,
):
    pulse = lax.axis_index("pulse")
    ranged = lax.axis_index("range")
    z = pulse // 2
    core = pulse % 2
    gx = ranged // 4
    gy = ranged % 4
    other = 1 - core
    buddy = flipped(pulse, 1)
    q2 = flipped(pulse, 2)
    q4 = flipped(pulse, 4)
    q6 = flipped(q2, 4)

    def z_peer(k):
        return ((z + k) % 8) * 2 + core

    def r_peer(k):
        return ((gx + k // 4) % 4) * 4 + (gy + k % 4) % 4

    load = pltpu.make_async_copy(data_hbm, data, load_s)
    load.start()

    barrier = pltpu.get_barrier_semaphore()
    pl.semaphore_signal(barrier, inc=1, device_id={"pulse": buddy}, device_id_type=MESH)
    pl.semaphore_signal(barrier, inc=1, device_id={"pulse": q6}, device_id_type=MESH)
    for k in (1, 2, 6, 7):
        pl.semaphore_signal(barrier, inc=1, device_id={"pulse": z_peer(k)}, device_id_type=MESH)
    for k in range(1, 16):
        pl.semaphore_signal(barrier, inc=1, device_id={"range": r_peer(k)}, device_id_type=MESH)

    def fill(ref, level, source):
        tap = taps[level, source]
        slope = squint[level:level + 1, :]
        first = slope.astype(bf16).astype(f32)
        second = (slope - first).astype(bf16).astype(f32)
        third = slope - first - second
        ref[...] = jnp.concatenate([
            (tap % 256).astype(f32), (tap // 256).astype(f32), weights[level, source].astype(f32),
            first, second, third, jnp.zeros_like(slope)], axis=0).astype(bf16)

    fill(snd.at[0], 1, 1)
    fill(snd.at[1], 2, 1)
    fill(prm.at[4], 2, 0)
    fill(prm.at[0], 0, 0)
    fill(prm.at[1], 0, 1)
    fill(prm.at[2], 1, 0)
    rowid[...] = lax.broadcasted_iota(jnp.int32, (256, 256), 0).astype(f32).astype(bf16)

    def build(m, slot):
        for nt in range(4):
            cols = slice(256 * nt, 256 * nt + 256)
            rows = prm[m, :, cols].astype(f32)
            places = [rows[tap:tap + 1] + 256.0 * rows[4 + tap:5 + tap] for tap in range(4)]
            scales = [rows[8 + tap:9 + tap].astype(bf16) for tap in range(4)]
            for kb in range(4):
                val = jnp.zeros((256, 256), bf16)
                for tap in range(4):
                    here = rowid[...] == (places[tap] - 256.0 * kb).astype(bf16)
                    val = jnp.where(here, scales[tap], val)
                W[slot, 256 * kb:256 * kb + 256, cols] = val

    first_range = (ranged * COLS).astype(f32)

    def prepare_rotation(m):
        rows = prm[m].astype(f32)
        slope = rows[12:13] + rows[13:14] + rows[14:15]
        i8 = lax.broadcasted_iota(jnp.int32, (8, BEAMS), 0).astype(f32)
        c0, s0 = sincos(slope * ((i8 + first_range) * (1.0 / RANGES)))
        cf, sf = sincos(slope * (jnp.where(i8 < 1.0, 8.0, 128.0) * (1.0 / RANGES)))
        rb[m, 0, 0] = c0
        rb[m, 0, 1] = s0
        ch = cf[1:2]
        sh = sf[1:2]
        rb[m, 1, 0] = c0 * ch - s0 * sh
        rb[m, 1, 1] = s0 * ch + c0 * sh
        rs[m, 0] = jnp.broadcast_to(cf[0:1], (8, BEAMS))
        rs[m, 1] = jnp.broadcast_to(sf[0:1], (8, BEAMS))

    def rotate(src, m, half, dest, kind, re_at, im_at):
        for nt in range(4):
            cols = slice(256 * nt, 256 * nt + 256)
            c = rb[m, half, 0, :, cols]
            s = rb[m, half, 1, :, cols]
            c8 = rs[m, 0, :, cols]
            s8 = rs[m, 1, :, cols]
            for i in range(8):
                reals = []
                imags = []
                for e in range(2):
                    q = 16 * i + 8 * e
                    a = src[re_at + q:re_at + q + 8, cols]
                    b = src[im_at + q:im_at + q + 8, cols]
                    reals.append(c * a - s * b)
                    imags.append(s * a + c * b)
                    c, s = c * c8 - s * s8, s * c8 + c * s8
                q = 128 * half + 16 * i
                dest[q:q + 16, cols] = jnp.concatenate(reals, axis=0).astype(kind)
                dest[256 + q:272 + q, cols] = jnp.concatenate(imags, axis=0).astype(kind)

    def rotate_all(src, m, dest, kind):
        for half in range(2):
            rotate(src, m, half, dest, kind, 128 * half, 256 + 128 * half)

    first_angle = BEAMS * (core + 8 * (z // 4))

    def table_base():
        angle = lax.broadcasted_iota(jnp.int32, (16, BEAMS), 1) + first_angle
        up = lax.broadcasted_iota(jnp.int32, (16, BEAMS), 0)
        us[0], us[1] = sincos(((64 * up * angle) % ANGLES).astype(f32) * (1.0 / ANGLES))

    def table(k):
        a8 = lax.broadcasted_iota(jnp.int32, (8, BEAMS), 1) + first_angle
        v8 = 8 * lax.broadcasted_iota(jnp.int32, (8, BEAMS), 0) + k
        vc, vs = sincos(((v8 * a8) % ANGLES).astype(f32) * (1.0 / ANGLES))
        for pair in range(8):
            cs = []
            ss = []
            for u in (2 * pair, 2 * pair + 1):
                uc = us[0, u:u + 1, :]
                un = us[1, u:u + 1, :]
                cs.append(uc * vc - un * vs)
                ss.append(un * vc + uc * vs)
            tab[k, 16 * pair:16 * pair + 16, :] = jnp.concatenate(cs, axis=0).astype(bf16)
            tab[k, 128 + 16 * pair:144 + 16 * pair, :] = jnp.concatenate(ss, axis=0).astype(bf16)

    build(0, 0)
    prepare_rotation(0)
    table_base()

    load.wait()
    for t in range(2):
        dT[0, t * COLS:(t + 1) * COLS, :] = data[t].T

    pl.semaphore_wait(barrier, 21)

    part = pltpu.make_async_remote_copy(
        dT.at[0], dT.at[1], part_s, part_r, device_id={"pulse": buddy}, device_id_type=MESH)
    part.start()
    prm_copies = []
    for n, (src, slot, target) in enumerate((
        (snd.at[0], 3, q2), (snd.at[1], 5, q4), (prm.at[4], 6, q2), (snd.at[1], 7, q6))):
        copy = pltpu.make_async_remote_copy(
            src, prm.at[slot], prm_s.at[n], prm_r.at[n],
            device_id={"pulse": target}, device_id_type=MESH)
        copy.start()
        prm_copies.append(copy)

    acc[0] = jnp.dot(dT[0], W[0], preferred_element_type=f32)
    build(1, 1)
    prepare_rotation(2)
    table(0)
    part.wait()
    acc[1] = jnp.dot(dT[1], W[1], preferred_element_type=f32) + acc[0]
    build(2, 0)
    table(1)
    rotate_all(acc.at[1], 0, S1, bf16)

    acc[0] = jnp.dot(S1[...], W[0], preferred_element_type=f32)
    prm_copies[0].wait()
    build(3, 1)
    prepare_rotation(3)
    table(2)

    acc[1] = jnp.dot(S1[...], W[1], preferred_element_type=f32)
    build(4, 0)
    rotate_all(acc.at[0], 2, U.at[0], bf16)
    prepare_rotation(4)
    table(3)

    bit0 = z % 2
    bit1 = (z // 2) % 2

    def slot_of(i):
        at0 = bit0 if i % 2 == 0 else 1 - bit0
        at1 = bit1 if i // 2 == 0 else 1 - bit1
        return at0 + 2 * at1

    acc[0] = jnp.dot(U[0], W[0], preferred_element_type=f32)
    prm_copies[1].wait()
    build(5, 1)
    rotate_all(acc.at[1], 3, U.at[1], bf16)
    prepare_rotation(5)
    table(4)

    acc[1] = jnp.dot(U[0], W[1], preferred_element_type=f32)
    prm_copies[2].wait()
    build(6, 0)
    rotate_all(acc.at[0], 4, X.at[slot_of(0)], f32)
    prepare_rotation(6)
    table(5)

    acc[0] = jnp.dot(U[1], W[0], preferred_element_type=f32)
    prm_copies[3].wait()
    build(7, 1)
    rotate_all(acc.at[1], 5, X.at[slot_of(2)], f32)
    prepare_rotation(7)
    table(6)

    def last(half):
        lhs = jnp.concatenate(
            [U[1, 128 * half:128 * half + 128, :], U[1, 256 + 128 * half:384 + 128 * half, :]], axis=0)
        acc[1, 256 * half:256 * half + 256, :] = jnp.dot(lhs, W[1], preferred_element_type=f32)

    root = math.sqrt(0.5)

    def combine(half, nt):
        cols = slice(256 * nt, 256 * nt + 256)
        for step in range(8):
            top = slice(128 * half + 16 * step, 128 * half + 16 * step + 16)
            low = slice(256 + 128 * half + 16 * step, 272 + 128 * half + 16 * step)
            xr = [X[n, top, cols] for n in range(4)]
            xi = [X[n, low, cols] for n in range(4)]
            e = [
                (xr[0] + xr[2], xi[0] + xi[2]),
                (xr[0] + xi[2], xi[0] - xr[2]),
                (xr[0] - xr[2], xi[0] - xi[2]),
                (xr[0] - xi[2], xi[0] + xr[2]),
            ]
            o = [
                (xr[1] + xr[3], xi[1] + xi[3]),
                (xr[1] + xi[3], xi[1] - xr[3]),
                (xr[1] - xr[3], xi[1] - xi[3]),
                (xr[1] - xi[3], xi[1] + xr[3]),
            ]
            t = [
                o[0],
                (root * (o[1][0] + o[1][1]), root * (o[1][1] - o[1][0])),
                (o[2][1], -o[2][0]),
                (root * (o[3][1] - o[3][0]), -root * (o[3][0] + o[3][1])),
            ]
            top = slice(16 * step, 16 * step + 16)
            low = slice(128 + 16 * step, 144 + 16 * step)
            for k in range(4):
                Y[half, k, top, cols] = (e[k][0] + t[k][0]).astype(bf16)
                Y[half, k, low, cols] = (e[k][1] + t[k][1]).astype(bf16)
                Y[half, k + 4, top, cols] = (e[k][0] - t[k][0]).astype(bf16)
                Y[half, k + 4, low, cols] = (e[k][1] - t[k][1]).astype(bf16)

    scale = ANGLES ** (-0.5)

    def spectrum(piece, beside):
        half = piece // 2
        for j in range(2):
            kk = 2 * (piece % 2) + j
            res = []
            ims = []
            for k in (2 * kk, 2 * kk + 1):
                both = lax.dot_general(tab[k], Y[half, k], NT, preferred_element_type=f32)
                res.append((both[:128, :128] + both[128:, 128:]) * scale)
                ims.append((both[:128, 128:] - both[128:, :128]) * scale)
            for t, parts in enumerate((res, ims)):
                val = jnp.concatenate([p.reshape(16, 8, 128) for p in parts], axis=1)
                val = val.reshape(8, 2, 16, 128)
                for c in range(2):
                    fst[piece, c, :, j, t] = val[:, c]
                    stg[piece, c, :, j, t] = val[:, c].astype(bf16)
            if beside is not None:
                combine(beside, kk)

    def to(src, dst, send, recv, target):
        return pltpu.make_async_remote_copy(
            src, dst, send, recv, device_id={"pulse": target}, device_id_type=MESH)

    def pair(piece):
        return to(stg.at[piece, other], prx.at[piece], pair_s.at[piece], pair_r.at[piece], buddy)

    def at(k):
        return (z + k) % 8

    def near_copy(piece, n):
        return to(zsn.at[piece, at((3, 5)[n])], near.at[piece, n],
                  near_s.at[piece, n], near_r.at[piece, n], z_peer((1, 7)[n]))

    def far_copy(piece, n):
        return to(zsn.at[piece, at(4), :, n], far.at[piece, n],
                  far_s.at[piece, n], far_r.at[piece, n], z_peer((2, 6)[n]))

    def z_copy(piece, n):
        src = cmb.at[piece, n] if n < 2 else zsn.at[piece, at((1, 7)[n - 2])]
        return to(src, zrx.at[piece, n], z_s.at[piece, n], z_r.at[piece, n], z_peer((2, 6, 1, 7)[n]))

    def relay(piece):
        pair(piece).wait()
        for d in range(8):
            both = fst[piece, core, d] + prx[piece, d].astype(f32)
            fst[piece, core, d] = both
            zsn[piece, d] = both.astype(bf16)
        for n in range(2):
            far_copy(piece, n).start()
        for n in range(2):
            near_copy(piece, n).start()
        for n in range(2, 4):
            z_copy(piece, n).start()

    def scatter(piece):
        for n in range(2):
            far_copy(piece, n).wait()
            near_copy(piece, n).wait()
            dest = at((2, 6)[n])
            for j in range(2):
                for t in range(2):
                    both = fst[piece, core, dest, j, t] + near[piece, n, j, t].astype(f32)
                    if t == n:
                        both = both + far[piece, n, j].astype(f32)
                    cmb[piece, n, j, t] = both.astype(bf16)
            z_copy(piece, n).start()

    last(0)
    rotate_all(acc.at[0], 6, X.at[slot_of(1)], f32)
    table(7)
    rotate(acc.at[1], 7, 0, X.at[slot_of(3)], f32, 0, 128)
    last(1)
    for nt in range(4):
        combine(0, nt)
    rotate(acc.at[1], 7, 1, X.at[slot_of(3)], f32, 256, 384)
    spectrum(0, 1)
    pair(0).start()
    spectrum(1, 1)
    pair(1).start()
    relay(0)
    spectrum(2, None)
    pair(2).start()
    relay(1)
    scatter(0)
    spectrum(3, None)
    pair(3).start()
    relay(2)
    scatter(1)
    relay(3)
    scatter(2)
    scatter(3)

    for piece in range(4):
        total = fst[piece, core, z]
        for n in range(4):
            z_copy(piece, n).wait()
            total = total + zrx[piece, n].astype(f32)
        for j in range(2):
            kk = 2 * (piece % 2) + j
            for t in range(2):
                here = 128 * (piece // 2)
                G[64 * t + 16 * kk:64 * t + 16 * kk + 16, here:here + 128] = total[j, t]

    gg = G[...]
    m = lax.dot_general(gg, gg, NT, precision=lax.Precision.HIGHEST, preferred_element_type=f32)
    lane = lax.broadcasted_iota(jnp.int32, (64, 128), 1)
    row = lax.broadcasted_iota(jnp.int32, (64, 128), 0)
    sign = jnp.where(lane < 64, 1.0, -1.0).astype(f32)
    cov = m[:64] * sign + pltpu.roll(m[64:], 64, 1)
    packed = jnp.where(lane <= row, cov, pltpu.roll(cov, 64, 1))
    packed = jnp.where(lane[:32] < 64, packed[:32], pltpu.roll(packed[32:], 64, 1))

    cx[ranged] = packed
    copies = []
    for k in (10, 9, 11, 6, 14, 2, 8, 5, 7, 13, 15, 1, 3, 4, 12):
        copy = pltpu.make_async_remote_copy(
            cx.at[ranged], cx.at[ranged], c_s.at[k - 1], c_r.at[k - 1],
            device_id={"range": r_peer(k)}, device_id_type=MESH)
        copy.start()
        copies.append(copy)
    for copy in copies:
        copy.wait()
    sums = [cx[n] for n in range(16)]
    while len(sums) > 1:
        sums = [sums[n] + sums[n + 1] for n in range(0, len(sums), 2)]
    packed = jnp.concatenate([sums[0], pltpu.roll(sums[0], 64, 1)], axis=0)
    square = jnp.concatenate([packed, packed], axis=0)
    flip = square.T[:64]
    c_re = jnp.where(lane <= row, packed, flip)
    c_im = jnp.where(lane > row, packed, jnp.where(lane < row, -flip, 0.0))

    K = jnp.concatenate([
        jnp.where(lane < 64, c_re, -pltpu.roll(c_im, 64, 1)),
        jnp.where(lane < 64, c_im, pltpu.roll(c_re, 64, 1)),
    ], axis=0)
    wide = lax.broadcasted_iota(jnp.int32, (128, 128), 1)
    w = jnp.sum(jnp.where(wide < 64, K, 0.0), axis=1, keepdims=True)
    v = w / jnp.sqrt(jnp.sum(w * w, axis=0, keepdims=True) + EPSILON)
    w = jnp.sum(K * v, axis=0, keepdims=True)
    v = w / jnp.sqrt(jnp.sum(w * w, axis=1, keepdims=True) + EPSILON)
    w = jnp.sum(K * v, axis=1, keepdims=True)
    v = w / jnp.sqrt(jnp.sum(w * w, axis=0, keepdims=True) + EPSILON)
    v = v * math.sqrt(BLOCK)
    vr = v[:64]
    vi = v[64:]
    gr = gg[:64]
    gi = gg[64:]
    focused = (gr * vr + gi * vi, gi * vr - gr * vi)
    for t in range(2):
        for k in range(8):
            for half in range(2):
                F[t, half, pl.ds(k, 8, stride=8), :] = focused[t][8 * k:8 * k + 8, 128 * half:128 * half + 128]
        for half in range(2):
            out[t, :, 128 * half:128 * half + 128] = F[t, half]


def per_device(pulse_data, merge_taps, merge_weights, squint):
    vmem = pl.BlockSpec(memory_space=pltpu.VMEM)
    dma = pltpu.SemaphoreType.DMA
    return pl.pallas_call(
        kernel,
        out_shape=jax.ShapeDtypeStruct((2, BLOCK, COLS), f32),
        in_specs=[pl.BlockSpec(memory_space=pl.ANY)] + [vmem] * 3,
        out_specs=vmem,
        scratch_shapes=[
            pltpu.VMEM((2, BEAMS, COLS), bf16),
            pltpu.VMEM((2, 512, BEAMS), bf16),
            pltpu.VMEM((8, 16, BEAMS), bf16),
            pltpu.VMEM((2, 16, BEAMS), bf16),
            pltpu.VMEM((2, BEAMS, BEAMS), bf16),
            pltpu.VMEM((256, 256), bf16),
            pltpu.VMEM((8, 2, 2, 8, BEAMS), f32),
            pltpu.VMEM((8, 2, 8, BEAMS), f32),
            pltpu.VMEM((2, 512, BEAMS), f32),
            pltpu.VMEM((512, BEAMS), bf16),
            pltpu.VMEM((2, 512, BEAMS), bf16),
            pltpu.VMEM((4, 512, BEAMS), f32),
            pltpu.VMEM((2, 8, 256, BEAMS), bf16),
            pltpu.VMEM((2, 16, BEAMS), f32),
            pltpu.VMEM((8, 256, BEAMS), bf16),
            pltpu.VMEM((4, 2, 8, 2, 2, 16, 128), f32),
            pltpu.VMEM((4, 2, 8, 2, 2, 16, 128), bf16),
            pltpu.VMEM((4, 8, 2, 2, 16, 128), bf16),
            pltpu.VMEM((4, 8, 2, 2, 16, 128), bf16),
            pltpu.VMEM((4, 2, 2, 2, 16, 128), bf16),
            pltpu.VMEM((4, 2, 2, 16, 128), bf16),
            pltpu.VMEM((4, 2, 2, 2, 16, 128), bf16),
            pltpu.VMEM((4, 4, 2, 2, 16, 128), bf16),
            pltpu.VMEM((128, COLS), f32),
            pltpu.VMEM((2, 2, 64, 128), f32),
            pltpu.VMEM((16, 32, 128), f32),
            dma, dma, dma,
            dma((4,)), dma((4,)),
            dma((4,)), dma((4,)),
            dma((4, 2)), dma((4, 2)),
            dma((4, 2)), dma((4, 2)),
            dma((4, 4)), dma((4, 4)),
            dma((15,)), dma((15,)),
        ],
        compiler_params=pltpu.CompilerParams(
            collective_id=0, has_side_effects=True, vmem_limit_bytes=60 * 1024 * 1024),
    )(pulse_data, merge_taps, merge_weights, squint)


def solution(mesh):
    placed = (
        P(None, "pulse", "range"),
        P(None, None, None, "pulse"),
        P(None, None, None, "pulse"),
        P(None, "pulse"),
    )
    return jax.shard_map(
        per_device, mesh=mesh, in_specs=placed, out_specs=P(None, "pulse", "range"), check_vma=False
    )
```

```python
import math

import jax
import jax.numpy as jnp
from jax import lax
from jax.experimental import pallas as pl
from jax.experimental.pallas import tpu as pltpu
from jax.sharding import PartitionSpec as P

RANGES = 4096
ANGLES = 16384
BEAMS = 1024
COLS = 256
BLOCK = 64
EPSILON = 1e-06
TWO_PI = 2.0 * math.pi
COS_TERMS = [(-1) ** k * TWO_PI ** (2 * k) / math.factorial(2 * k) for k in range(10)]
SIN_TERMS = [(-1) ** k * TWO_PI ** (2 * k + 1) / math.factorial(2 * k + 1) for k in range(9)]
MESH = pl.DeviceIdType.MESH
f32 = jnp.float32
bf16 = jnp.bfloat16
NT = (((1,), (1,)), ((), ()))
STEPS = (4, 3, 5, 0, 1, 2, 6, 7)


def flipped(index, bit):
    return index + bit - 2 * bit * ((index // bit) % 2)


def sincos(turns):
    part = turns - jnp.floor(turns + 0.5)
    y = part * part
    c = jnp.full_like(y, COS_TERMS[-1])
    for term in COS_TERMS[-2::-1]:
        c = c * y + term
    s = jnp.full_like(y, SIN_TERMS[-1])
    for term in SIN_TERMS[-2::-1]:
        s = s * y + term
    return c, s * part


def kernel(
    data_hbm, taps, weights, squint, out,
    data, dT, prm, snd, W, rowid, rb, rs, acc, S1, U, X, Y, us, tab,
    fst, stg, prx, zsn, near, far, zrx, G, F, cx,
    load_s, part_s, part_r, prm_s, prm_r, pair_s, pair_r,
    near_s, near_r, far_s, far_r, z_s, z_r, c_s, c_r,
):
    pulse = lax.axis_index("pulse")
    ranged = lax.axis_index("range")
    z = pulse // 2
    core = pulse % 2
    gx = ranged // 4
    gy = ranged % 4
    other = 1 - core
    buddy = flipped(pulse, 1)
    q2 = flipped(pulse, 2)
    q4 = flipped(pulse, 4)
    q6 = flipped(q2, 4)

    def z_peer(k):
        return ((z + k) % 8) * 2 + core

    def r_peer(k):
        return ((gx + k // 4) % 4) * 4 + (gy + k % 4) % 4

    load = pltpu.make_async_copy(data_hbm, data, load_s)
    load.start()

    barrier = pltpu.get_barrier_semaphore()
    pl.semaphore_signal(barrier, inc=1, device_id={"pulse": buddy}, device_id_type=MESH)
    pl.semaphore_signal(barrier, inc=1, device_id={"pulse": q6}, device_id_type=MESH)
    for k in (1, 2, 6, 7):
        pl.semaphore_signal(barrier, inc=1, device_id={"pulse": z_peer(k)}, device_id_type=MESH)
    for k in range(1, 16):
        pl.semaphore_signal(barrier, inc=1, device_id={"range": r_peer(k)}, device_id_type=MESH)

    def fill(ref, level, source):
        tap = taps[level, source]
        slope = squint[level:level + 1, :]
        first = slope.astype(bf16).astype(f32)
        second = (slope - first).astype(bf16).astype(f32)
        third = slope - first - second
        ref[...] = jnp.concatenate([
            (tap % 256).astype(f32), (tap // 256).astype(f32), weights[level, source].astype(f32),
            first, second, third, jnp.zeros_like(slope)], axis=0).astype(bf16)

    fill(snd.at[0], 1, 1)
    fill(snd.at[1], 2, 1)
    fill(prm.at[4], 2, 0)
    fill(prm.at[0], 0, 0)
    fill(prm.at[1], 0, 1)
    fill(prm.at[2], 1, 0)
    rowid[...] = lax.broadcasted_iota(jnp.int32, (256, 256), 0).astype(f32).astype(bf16)

    def build(m, slot):
        for nt in range(4):
            cols = slice(256 * nt, 256 * nt + 256)
            rows = prm[m, :, cols].astype(f32)
            places = [rows[tap:tap + 1] + 256.0 * rows[4 + tap:5 + tap] for tap in range(4)]
            scales = [rows[8 + tap:9 + tap].astype(bf16) for tap in range(4)]
            for kb in range(4):
                val = jnp.zeros((256, 256), bf16)
                for tap in range(4):
                    here = rowid[...] == (places[tap] - 256.0 * kb).astype(bf16)
                    val = jnp.where(here, scales[tap], val)
                W[slot, 256 * kb:256 * kb + 256, cols] = val

    first_range = (ranged * COLS).astype(f32)

    def prepare_rotation(m):
        rows = prm[m].astype(f32)
        slope = rows[12:13] + rows[13:14] + rows[14:15]
        i8 = lax.broadcasted_iota(jnp.int32, (8, BEAMS), 0).astype(f32)
        c0, s0 = sincos(slope * ((i8 + first_range) * (1.0 / RANGES)))
        cf, sf = sincos(slope * (jnp.where(i8 < 1.0, 8.0, 128.0) * (1.0 / RANGES)))
        rb[m, 0, 0] = c0
        rb[m, 0, 1] = s0
        ch = cf[1:2]
        sh = sf[1:2]
        rb[m, 1, 0] = c0 * ch - s0 * sh
        rb[m, 1, 1] = s0 * ch + c0 * sh
        rs[m, 0] = jnp.broadcast_to(cf[0:1], (8, BEAMS))
        rs[m, 1] = jnp.broadcast_to(sf[0:1], (8, BEAMS))

    def rotate(src, m, half, dest, kind, re_at, im_at):
        for nt in range(4):
            cols = slice(256 * nt, 256 * nt + 256)
            c = rb[m, half, 0, :, cols]
            s = rb[m, half, 1, :, cols]
            c8 = rs[m, 0, :, cols]
            s8 = rs[m, 1, :, cols]
            for i in range(8):
                reals = []
                imags = []
                for e in range(2):
                    q = 16 * i + 8 * e
                    a = src[re_at + q:re_at + q + 8, cols]
                    b = src[im_at + q:im_at + q + 8, cols]
                    reals.append(c * a - s * b)
                    imags.append(s * a + c * b)
                    c, s = c * c8 - s * s8, s * c8 + c * s8
                q = 128 * half + 16 * i
                dest[q:q + 16, cols] = jnp.concatenate(reals, axis=0).astype(kind)
                dest[256 + q:272 + q, cols] = jnp.concatenate(imags, axis=0).astype(kind)

    def rotate_all(src, m, dest, kind):
        for half in range(2):
            rotate(src, m, half, dest, kind, 128 * half, 256 + 128 * half)

    first_angle = BEAMS * (core + 8 * (z // 4))

    def table_base():
        angle = lax.broadcasted_iota(jnp.int32, (1, BEAMS), 1) + first_angle
        rows = []
        for step in STEPS:
            for c in (core, other):
                rows.append(angle * (64 * (((z + step) % 8) * 2 + c)))
        us[0], us[1] = sincos((jnp.concatenate(rows, axis=0) % ANGLES).astype(f32) * (1.0 / ANGLES))

    def table(k):
        a8 = lax.broadcasted_iota(jnp.int32, (8, BEAMS), 1) + first_angle
        v8 = 8 * lax.broadcasted_iota(jnp.int32, (8, BEAMS), 0) + k
        vc, vs = sincos(((v8 * a8) % ANGLES).astype(f32) * (1.0 / ANGLES))
        for q in range(8):
            cs = []
            ss = []
            for u in (2 * q, 2 * q + 1):
                uc = us[0, u:u + 1, :]
                un = us[1, u:u + 1, :]
                cs.append(uc * vc - un * vs)
                ss.append(un * vc + uc * vs)
            at_c, at_s = (16 * q, 48 + 16 * q) if q < 3 else (48 + 16 * q, 128 + 16 * q)
            tab[k, at_c:at_c + 16, :] = jnp.concatenate(cs, axis=0).astype(bf16)
            tab[k, at_s:at_s + 16, :] = jnp.concatenate(ss, axis=0).astype(bf16)

    build(0, 0)

    load.wait()
    for t in range(2):
        dT[0, t * COLS:(t + 1) * COLS, :] = data[t].T

    pl.semaphore_wait(barrier, 21)

    part = pltpu.make_async_remote_copy(
        dT.at[0], dT.at[1], part_s, part_r, device_id={"pulse": buddy}, device_id_type=MESH)
    part.start()
    prm_copies = []
    for n, (src, slot, target) in enumerate((
        (snd.at[0], 3, q2), (snd.at[1], 5, q4), (prm.at[4], 6, q2), (snd.at[1], 7, q6))):
        copy = pltpu.make_async_remote_copy(
            src, prm.at[slot], prm_s.at[n], prm_r.at[n],
            device_id={"pulse": target}, device_id_type=MESH)
        copy.start()
        prm_copies.append(copy)

    acc[0] = jnp.dot(dT[0], W[0], preferred_element_type=f32)
    build(1, 1)
    prepare_rotation(0)
    table_base()
    prepare_rotation(2)
    table(0)
    part.wait()
    acc[1] = jnp.dot(dT[1], W[1], preferred_element_type=f32) + acc[0]
    build(2, 0)
    table(1)
    rotate_all(acc.at[1], 0, S1, bf16)

    acc[0] = jnp.dot(S1[...], W[0], preferred_element_type=f32)
    prm_copies[0].wait()
    build(3, 1)
    prepare_rotation(3)
    table(2)

    acc[1] = jnp.dot(S1[...], W[1], preferred_element_type=f32)
    build(4, 0)
    rotate_all(acc.at[0], 2, U.at[0], bf16)
    prepare_rotation(4)
    table(3)

    bit0 = z % 2
    bit1 = (z // 2) % 2

    def slot_of(i):
        at0 = bit0 if i % 2 == 0 else 1 - bit0
        at1 = bit1 if i // 2 == 0 else 1 - bit1
        return at0 + 2 * at1

    acc[0] = jnp.dot(U[0], W[0], preferred_element_type=f32)
    prm_copies[1].wait()
    build(5, 1)
    rotate_all(acc.at[1], 3, U.at[1], bf16)
    prepare_rotation(5)
    table(4)

    acc[1] = jnp.dot(U[0], W[1], preferred_element_type=f32)
    prm_copies[2].wait()
    build(6, 0)
    rotate_all(acc.at[0], 4, X.at[slot_of(0)], f32)
    prepare_rotation(6)
    table(5)

    acc[0] = jnp.dot(U[1], W[0], preferred_element_type=f32)
    prm_copies[3].wait()
    build(7, 1)
    rotate_all(acc.at[1], 5, X.at[slot_of(2)], f32)
    prepare_rotation(7)
    table(6)

    def last(half):
        lhs = jnp.concatenate(
            [U[1, 128 * half:128 * half + 128, :], U[1, 256 + 128 * half:384 + 128 * half, :]], axis=0)
        acc[1, 256 * half:256 * half + 256, :] = jnp.dot(lhs, W[1], preferred_element_type=f32)

    root = math.sqrt(0.5)

    def combine(half, nt):
        cols = slice(256 * nt, 256 * nt + 256)
        for step in range(8):
            top = slice(128 * half + 16 * step, 128 * half + 16 * step + 16)
            low = slice(256 + 128 * half + 16 * step, 272 + 128 * half + 16 * step)
            xr = [X[n, top, cols] for n in range(4)]
            xi = [X[n, low, cols] for n in range(4)]
            e = [
                (xr[0] + xr[2], xi[0] + xi[2]),
                (xr[0] + xi[2], xi[0] - xr[2]),
                (xr[0] - xr[2], xi[0] - xi[2]),
                (xr[0] - xi[2], xi[0] + xr[2]),
            ]
            o = [
                (xr[1] + xr[3], xi[1] + xi[3]),
                (xr[1] + xi[3], xi[1] - xr[3]),
                (xr[1] - xr[3], xi[1] - xi[3]),
                (xr[1] - xi[3], xi[1] + xr[3]),
            ]
            t = [
                o[0],
                (root * (o[1][0] + o[1][1]), root * (o[1][1] - o[1][0])),
                (o[2][1], -o[2][0]),
                (root * (o[3][1] - o[3][0]), -root * (o[3][0] + o[3][1])),
            ]
            top = slice(16 * step, 16 * step + 16)
            low = slice(128 + 16 * step, 144 + 16 * step)
            for k in range(4):
                Y[half, k, top, cols] = (e[k][0] + t[k][0]).astype(bf16)
                Y[half, k, low, cols] = (e[k][1] + t[k][1]).astype(bf16)
                Y[half, k + 4, top, cols] = (e[k][0] - t[k][0]).astype(bf16)
                Y[half, k + 4, low, cols] = (e[k][1] - t[k][1]).astype(bf16)

    scale = ANGLES ** (-0.5)

    def spectrum(half, group, beside):
        lo, hi, size = ((0, 3, 48), (3, 8, 80))[group]
        first = 96 * group
        for kk in range(4):
            res = []
            ims = []
            for k in (2 * kk, 2 * kk + 1):
                both = lax.dot_general(
                    tab[k, first:first + 2 * size, :], Y[half, k], NT, preferred_element_type=f32)
                res.append((both[:size, :128] + both[size:, 128:]) * scale)
                ims.append((both[:size, 128:] - both[size:, :128]) * scale)
            for t, parts in enumerate((res, ims)):
                val = jnp.concatenate([p.reshape(size // 8, 8, 128) for p in parts], axis=1)
                val = val.reshape(hi - lo, 2, 16, 128)
                fst[half, lo:hi, kk, t] = val[:, 0]
                stg[half, lo:hi, kk, t] = val[:, 1].astype(bf16)
            if beside is not None:
                combine(beside, kk)

    def to(src, dst, send, recv, target):
        return pltpu.make_async_remote_copy(
            src, dst, send, recv, device_id={"pulse": target}, device_id_type=MESH)

    def pair(half, group):
        lo, size = ((0, 3), (3, 5))[group]
        return to(stg.at[half, pl.ds(lo, size)], prx.at[half, pl.ds(lo, size)],
                  pair_s.at[half, group], pair_r.at[half, group], buddy)

    def near_copy(half, n):
        return to(zsn.at[half, 1 + n], near.at[half, n],
                  near_s.at[half, n], near_r.at[half, n], z_peer((1, 7)[n]))

    def far_copy(half, n):
        return to(zsn.at[half, 0, :, n], far.at[half, n],
                  far_s.at[half, n], far_r.at[half, n], z_peer((2, 6)[n]))

    def z_copy(half, n):
        return to(zsn.at[half, (5, 6, 4, 7)[n]], zrx.at[half, n],
                  z_s.at[half, n], z_r.at[half, n], z_peer((2, 6, 1, 7)[n]))

    def relay(half):
        pair(half, 0).wait()
        for q in range(3):
            zsn[half, q] = (fst[half, q] + prx[half, q].astype(f32)).astype(bf16)
        for n in range(2):
            far_copy(half, n).start()
        for n in range(2):
            near_copy(half, n).start()

    def scatter(half):
        pair(half, 1).wait()
        for n in (2, 3):
            q = (5, 6, 4, 7)[n]
            zsn[half, q] = (fst[half, q] + prx[half, q].astype(f32)).astype(bf16)
            z_copy(half, n).start()
        fst[half, 3] = fst[half, 3] + prx[half, 3].astype(f32)
        for n in (0, 1):
            far_copy(half, n).wait()
            near_copy(half, n).wait()
            q = 5 + n
            for t in range(2):
                both = fst[half, q, :, t] + prx[half, q, :, t].astype(f32) + near[half, n, :, t].astype(f32)
                if t == n:
                    both = both + far[half, n].astype(f32)
                zsn[half, q, :, t] = both.astype(bf16)
            z_copy(half, n).start()

    last(0)
    rotate_all(acc.at[0], 6, X.at[slot_of(1)], f32)
    table(7)
    rotate(acc.at[1], 7, 0, X.at[slot_of(3)], f32, 0, 128)
    last(1)
    for nt in range(4):
        combine(0, nt)
    rotate(acc.at[1], 7, 1, X.at[slot_of(3)], f32, 256, 384)
    spectrum(0, 0, 1)
    pair(0, 0).start()
    spectrum(1, 0, None)
    pair(1, 0).start()
    relay(0)
    spectrum(0, 1, None)
    pair(0, 1).start()
    relay(1)
    spectrum(1, 1, None)
    pair(1, 1).start()
    scatter(0)
    scatter(1)

    for half in range(2):
        total = fst[half, 3]
        for n in (2, 3, 0, 1):
            z_copy(half, n).wait()
            total = total + zrx[half, n].astype(f32)
        for kk in range(4):
            for t in range(2):
                G[64 * t + 16 * kk:64 * t + 16 * kk + 16, 128 * half:128 * half + 128] = total[kk, t]

    gg = G[...]
    m = lax.dot_general(gg, gg, NT, precision=lax.Precision.HIGHEST, preferred_element_type=f32)
    lane = lax.broadcasted_iota(jnp.int32, (64, 128), 1)
    row = lax.broadcasted_iota(jnp.int32, (64, 128), 0)
    sign = jnp.where(lane < 64, 1.0, -1.0).astype(f32)
    cov = m[:64] * sign + pltpu.roll(m[64:], 64, 1)
    packed = jnp.where(lane <= row, cov, pltpu.roll(cov, 64, 1))
    packed = jnp.where(lane[:32] < 64, packed[:32], pltpu.roll(packed[32:], 64, 1))

    cx[ranged] = packed
    copies = []
    for k in (10, 9, 11, 6, 14, 2, 8, 5, 7, 13, 15, 1, 3, 4, 12):
        copy = pltpu.make_async_remote_copy(
            cx.at[ranged], cx.at[ranged], c_s.at[k - 1], c_r.at[k - 1],
            device_id={"range": r_peer(k)}, device_id_type=MESH)
        copy.start()
        copies.append(copy)
    for copy in copies:
        copy.wait()
    sums = [cx[n] for n in range(16)]
    while len(sums) > 1:
        sums = [sums[n] + sums[n + 1] for n in range(0, len(sums), 2)]
    packed = jnp.concatenate([sums[0], pltpu.roll(sums[0], 64, 1)], axis=0)
    square = jnp.concatenate([packed, packed], axis=0)
    flip = square.T[:64]
    c_re = jnp.where(lane <= row, packed, flip)
    c_im = jnp.where(lane > row, packed, jnp.where(lane < row, -flip, 0.0))

    K = jnp.concatenate([
        jnp.where(lane < 64, c_re, -pltpu.roll(c_im, 64, 1)),
        jnp.where(lane < 64, c_im, pltpu.roll(c_re, 64, 1)),
    ], axis=0)
    wide = lax.broadcasted_iota(jnp.int32, (128, 128), 1)
    w = jnp.sum(jnp.where(wide < 64, K, 0.0), axis=1, keepdims=True)
    v = w / jnp.sqrt(jnp.sum(w * w, axis=0, keepdims=True) + EPSILON)
    w = jnp.sum(K * v, axis=0, keepdims=True)
    v = w / jnp.sqrt(jnp.sum(w * w, axis=1, keepdims=True) + EPSILON)
    w = jnp.sum(K * v, axis=1, keepdims=True)
    v = w / jnp.sqrt(jnp.sum(w * w, axis=0, keepdims=True) + EPSILON)
    v = v * math.sqrt(BLOCK)
    vr = v[:64]
    vi = v[64:]
    gr = gg[:64]
    gi = gg[64:]
    focused = (gr * vr + gi * vi, gi * vr - gr * vi)
    for t in range(2):
        for k in range(8):
            for half in range(2):
                F[t, half, pl.ds(k, 8, stride=8), :] = focused[t][8 * k:8 * k + 8, 128 * half:128 * half + 128]
        for half in range(2):
            out[t, :, 128 * half:128 * half + 128] = F[t, half]


def per_device(pulse_data, merge_taps, merge_weights, squint):
    vmem = pl.BlockSpec(memory_space=pltpu.VMEM)
    dma = pltpu.SemaphoreType.DMA
    return pl.pallas_call(
        kernel,
        out_shape=jax.ShapeDtypeStruct((2, BLOCK, COLS), f32),
        in_specs=[pl.BlockSpec(memory_space=pl.ANY)] + [vmem] * 3,
        out_specs=vmem,
        scratch_shapes=[
            pltpu.VMEM((2, BEAMS, COLS), bf16),
            pltpu.VMEM((2, 512, BEAMS), bf16),
            pltpu.VMEM((8, 16, BEAMS), bf16),
            pltpu.VMEM((2, 16, BEAMS), bf16),
            pltpu.VMEM((2, BEAMS, BEAMS), bf16),
            pltpu.VMEM((256, 256), bf16),
            pltpu.VMEM((8, 2, 2, 8, BEAMS), f32),
            pltpu.VMEM((8, 2, 8, BEAMS), f32),
            pltpu.VMEM((2, 512, BEAMS), f32),
            pltpu.VMEM((512, BEAMS), bf16),
            pltpu.VMEM((2, 512, BEAMS), bf16),
            pltpu.VMEM((4, 512, BEAMS), f32),
            pltpu.VMEM((2, 8, 256, BEAMS), bf16),
            pltpu.VMEM((2, 16, BEAMS), f32),
            pltpu.VMEM((8, 256, BEAMS), bf16),
            pltpu.VMEM((2, 8, 4, 2, 16, 128), f32),
            pltpu.VMEM((2, 8, 4, 2, 16, 128), bf16),
            pltpu.VMEM((2, 8, 4, 2, 16, 128), bf16),
            pltpu.VMEM((2, 8, 4, 2, 16, 128), bf16),
            pltpu.VMEM((2, 2, 4, 2, 16, 128), bf16),
            pltpu.VMEM((2, 2, 4, 16, 128), bf16),
            pltpu.VMEM((2, 4, 4, 2, 16, 128), bf16),
            pltpu.VMEM((128, COLS), f32),
            pltpu.VMEM((2, 2, 64, 128), f32),
            pltpu.VMEM((16, 32, 128), f32),
            dma, dma, dma,
            dma((4,)), dma((4,)),
            dma((2, 2)), dma((2, 2)),
            dma((2, 2)), dma((2, 2)),
            dma((2, 2)), dma((2, 2)),
            dma((2, 4)), dma((2, 4)),
            dma((15,)), dma((15,)),
        ],
        compiler_params=pltpu.CompilerParams(
            collective_id=0, has_side_effects=True, vmem_limit_bytes=60 * 1024 * 1024),
    )(pulse_data, merge_taps, merge_weights, squint)


def solution(mesh):
    placed = (
        P(None, "pulse", "range"),
        P(None, None, None, "pulse"),
        P(None, None, None, "pulse"),
        P(None, "pulse"),
    )
    return jax.shard_map(
        per_device, mesh=mesh, in_specs=placed, out_specs=P(None, "pulse", "range"), check_vma=False
    )
```

```python
import math

import jax
import jax.numpy as jnp
from jax import lax
from jax.experimental import pallas as pl
from jax.experimental.pallas import tpu as pltpu
from jax.sharding import PartitionSpec as P

RANGES = 4096
ANGLES = 16384
BEAMS = 1024
COLS = 256
BLOCK = 64
EPSILON = 1e-06
TWO_PI = 2.0 * math.pi
COS_TERMS = [(-1) ** k * TWO_PI ** (2 * k) / math.factorial(2 * k) for k in range(10)]
SIN_TERMS = [(-1) ** k * TWO_PI ** (2 * k + 1) / math.factorial(2 * k + 1) for k in range(9)]
MESH = pl.DeviceIdType.MESH
f32 = jnp.float32
bf16 = jnp.bfloat16
NT = (((1,), (1,)), ((), ()))
STEPS = (4, 3, 5, 0, 1, 2, 6, 7)


def flipped(index, bit):
    return index + bit - 2 * bit * ((index // bit) % 2)


def sincos(turns):
    part = turns - jnp.floor(turns + 0.5)
    y = part * part
    c = jnp.full_like(y, COS_TERMS[-1])
    for term in COS_TERMS[-2::-1]:
        c = c * y + term
    s = jnp.full_like(y, SIN_TERMS[-1])
    for term in SIN_TERMS[-2::-1]:
        s = s * y + term
    return c, s * part


def kernel(
    data_hbm, taps, weights, squint, out,
    data, dT, prm, snd, W, rowid, rb, rs, acc, S1, U, X, Y, us, tab,
    fst, stg, prx, zsn, near, far, zrx, G, F, cx,
    load_s, part_s, part_r, prm_s, prm_r, pair_s, pair_r,
    near_s, near_r, far_s, far_r, z_s, z_r, c_s, c_r,
):
    pulse = lax.axis_index("pulse")
    ranged = lax.axis_index("range")
    z = pulse // 2
    core = pulse % 2
    gx = ranged // 4
    gy = ranged % 4
    other = 1 - core
    buddy = flipped(pulse, 1)
    q2 = flipped(pulse, 2)
    q4 = flipped(pulse, 4)
    q6 = flipped(q2, 4)

    def z_peer(k):
        return ((z + k) % 8) * 2 + core

    def r_peer(k):
        return ((gx + k // 4) % 4) * 4 + (gy + k % 4) % 4

    load = pltpu.make_async_copy(data_hbm, data, load_s)
    load.start()

    barrier = pltpu.get_barrier_semaphore()
    pl.semaphore_signal(barrier, inc=1, device_id={"pulse": buddy}, device_id_type=MESH)
    pl.semaphore_signal(barrier, inc=1, device_id={"pulse": q6}, device_id_type=MESH)
    for k in (1, 2, 6, 7):
        pl.semaphore_signal(barrier, inc=1, device_id={"pulse": z_peer(k)}, device_id_type=MESH)
    for k in range(1, 16):
        pl.semaphore_signal(barrier, inc=1, device_id={"range": r_peer(k)}, device_id_type=MESH)

    def fill(ref, level, source):
        tap = taps[level, source]
        slope = squint[level:level + 1, :]
        first = slope.astype(bf16).astype(f32)
        second = (slope - first).astype(bf16).astype(f32)
        third = slope - first - second
        ref[...] = jnp.concatenate([
            (tap % 256).astype(f32), (tap // 256).astype(f32), weights[level, source].astype(f32),
            first, second, third, jnp.zeros_like(slope)], axis=0).astype(bf16)

    fill(snd.at[0], 1, 1)
    fill(snd.at[1], 2, 1)
    fill(prm.at[4], 2, 0)
    fill(prm.at[0], 0, 0)
    fill(prm.at[1], 0, 1)
    fill(prm.at[2], 1, 0)
    rowid[...] = lax.broadcasted_iota(jnp.int32, (256, 256), 0).astype(f32).astype(bf16)

    def build(m, slot):
        for nt in range(4):
            cols = slice(256 * nt, 256 * nt + 256)
            rows = prm[m, :, cols].astype(f32)
            places = [rows[tap:tap + 1] + 256.0 * rows[4 + tap:5 + tap] for tap in range(4)]
            scales = [rows[8 + tap:9 + tap].astype(bf16) for tap in range(4)]
            for kb in range(4):
                val = jnp.zeros((256, 256), bf16)
                for tap in range(4):
                    here = rowid[...] == (places[tap] - 256.0 * kb).astype(bf16)
                    val = jnp.where(here, scales[tap], val)
                W[slot, 256 * kb:256 * kb + 256, cols] = val

    first_range = (ranged * COLS).astype(f32)

    def prepare_rotation(m):
        rows = prm[m].astype(f32)
        slope = rows[12:13] + rows[13:14] + rows[14:15]
        i8 = lax.broadcasted_iota(jnp.int32, (8, BEAMS), 0).astype(f32)
        c0, s0 = sincos(slope * ((i8 + first_range) * (1.0 / RANGES)))
        cf, sf = sincos(slope * (jnp.where(i8 < 1.0, 8.0, 128.0) * (1.0 / RANGES)))
        rb[m, 0, 0] = c0
        rb[m, 0, 1] = s0
        ch = cf[1:2]
        sh = sf[1:2]
        rb[m, 1, 0] = c0 * ch - s0 * sh
        rb[m, 1, 1] = s0 * ch + c0 * sh
        rs[m, 0] = jnp.broadcast_to(cf[0:1], (8, BEAMS))
        rs[m, 1] = jnp.broadcast_to(sf[0:1], (8, BEAMS))

    def rotate(src, m, half, dest, kind, re_at, im_at):
        for nt in range(4):
            cols = slice(256 * nt, 256 * nt + 256)
            c = rb[m, half, 0, :, cols]
            s = rb[m, half, 1, :, cols]
            c8 = rs[m, 0, :, cols]
            s8 = rs[m, 1, :, cols]
            for i in range(8):
                reals = []
                imags = []
                for e in range(2):
                    q = 16 * i + 8 * e
                    a = src[re_at + q:re_at + q + 8, cols]
                    b = src[im_at + q:im_at + q + 8, cols]
                    reals.append(c * a - s * b)
                    imags.append(s * a + c * b)
                    c, s = c * c8 - s * s8, s * c8 + c * s8
                q = 128 * half + 16 * i
                dest[q:q + 16, cols] = jnp.concatenate(reals, axis=0).astype(kind)
                dest[256 + q:272 + q, cols] = jnp.concatenate(imags, axis=0).astype(kind)

    def rotate_all(src, m, dest, kind):
        for half in range(2):
            rotate(src, m, half, dest, kind, 128 * half, 256 + 128 * half)

    first_angle = BEAMS * (core + 8 * (z // 4))

    def table_base():
        angle = lax.broadcasted_iota(jnp.int32, (1, BEAMS), 1) + first_angle
        rows = []
        for step in STEPS:
            for c in (core, other):
                rows.append(angle * (64 * (((z + step) % 8) * 2 + c)))
        us[0], us[1] = sincos((jnp.concatenate(rows, axis=0) % ANGLES).astype(f32) * (1.0 / ANGLES))

    def table(k):
        a8 = lax.broadcasted_iota(jnp.int32, (8, BEAMS), 1) + first_angle
        v8 = 8 * lax.broadcasted_iota(jnp.int32, (8, BEAMS), 0) + k
        vc, vs = sincos(((v8 * a8) % ANGLES).astype(f32) * (1.0 / ANGLES))
        for q in range(8):
            cs = []
            ss = []
            for u in (2 * q, 2 * q + 1):
                uc = us[0, u:u + 1, :]
                un = us[1, u:u + 1, :]
                cs.append(uc * vc - un * vs)
                ss.append(un * vc + uc * vs)
            at_c, at_s = (16 * q, 48 + 16 * q) if q < 3 else (48 + 16 * q, 128 + 16 * q)
            tab[k, at_c:at_c + 16, :] = jnp.concatenate(cs, axis=0).astype(bf16)
            tab[k, at_s:at_s + 16, :] = jnp.concatenate(ss, axis=0).astype(bf16)

    build(0, 0)

    load.wait()
    for t in range(2):
        dT[0, t * COLS:(t + 1) * COLS, :] = data[t].T

    pl.semaphore_wait(barrier, 21)

    part = pltpu.make_async_remote_copy(
        dT.at[0], dT.at[1], part_s, part_r, device_id={"pulse": buddy}, device_id_type=MESH)
    part.start()
    prm_copies = []
    for n, (src, slot, target) in enumerate((
        (snd.at[0], 3, q2), (snd.at[1], 5, q4), (prm.at[4], 6, q2), (snd.at[1], 7, q6))):
        copy = pltpu.make_async_remote_copy(
            src, prm.at[slot], prm_s.at[n], prm_r.at[n],
            device_id={"pulse": target}, device_id_type=MESH)
        copy.start()
        prm_copies.append(copy)

    acc[0] = jnp.dot(dT[0], W[0], preferred_element_type=f32)
    build(1, 1)
    prepare_rotation(0)
    table_base()
    prepare_rotation(2)
    table(0)
    part.wait()
    acc[1] = jnp.dot(dT[1], W[1], preferred_element_type=f32) + acc[0]
    build(2, 0)
    table(1)
    rotate_all(acc.at[1], 0, S1, bf16)

    acc[0] = jnp.dot(S1[...], W[0], preferred_element_type=f32)
    prm_copies[0].wait()
    build(3, 1)
    prepare_rotation(3)
    table(2)

    acc[1] = jnp.dot(S1[...], W[1], preferred_element_type=f32)
    build(4, 0)
    rotate_all(acc.at[0], 2, U.at[0], bf16)
    prepare_rotation(4)
    table(3)

    bit0 = z % 2
    bit1 = (z // 2) % 2

    def slot_of(i):
        at0 = bit0 if i % 2 == 0 else 1 - bit0
        at1 = bit1 if i // 2 == 0 else 1 - bit1
        return at0 + 2 * at1

    acc[0] = jnp.dot(U[0], W[0], preferred_element_type=f32)
    prm_copies[1].wait()
    build(5, 1)
    rotate_all(acc.at[1], 3, U.at[1], bf16)
    prepare_rotation(5)
    table(4)

    acc[1] = jnp.dot(U[0], W[1], preferred_element_type=f32)
    prm_copies[2].wait()
    build(6, 0)
    rotate_all(acc.at[0], 4, X.at[slot_of(0)], f32)
    prepare_rotation(6)
    table(5)

    acc[0] = jnp.dot(U[1], W[0], preferred_element_type=f32)
    prm_copies[3].wait()
    build(7, 1)
    rotate_all(acc.at[1], 5, X.at[slot_of(2)], f32)
    prepare_rotation(7)
    table(6)

    def last(half):
        lhs = jnp.concatenate(
            [U[1, 128 * half:128 * half + 128, :], U[1, 256 + 128 * half:384 + 128 * half, :]], axis=0)
        acc[1, 256 * half:256 * half + 256, :] = jnp.dot(lhs, W[1], preferred_element_type=f32)

    root = math.sqrt(0.5)

    def combine(half, nt):
        cols = slice(256 * nt, 256 * nt + 256)
        for step in range(8):
            top = slice(128 * half + 16 * step, 128 * half + 16 * step + 16)
            low = slice(256 + 128 * half + 16 * step, 272 + 128 * half + 16 * step)
            xr = [X[n, top, cols] for n in range(4)]
            xi = [X[n, low, cols] for n in range(4)]
            e = [
                (xr[0] + xr[2], xi[0] + xi[2]),
                (xr[0] + xi[2], xi[0] - xr[2]),
                (xr[0] - xr[2], xi[0] - xi[2]),
                (xr[0] - xi[2], xi[0] + xr[2]),
            ]
            o = [
                (xr[1] + xr[3], xi[1] + xi[3]),
                (xr[1] + xi[3], xi[1] - xr[3]),
                (xr[1] - xr[3], xi[1] - xi[3]),
                (xr[1] - xi[3], xi[1] + xr[3]),
            ]
            t = [
                o[0],
                (root * (o[1][0] + o[1][1]), root * (o[1][1] - o[1][0])),
                (o[2][1], -o[2][0]),
                (root * (o[3][1] - o[3][0]), -root * (o[3][0] + o[3][1])),
            ]
            top = slice(16 * step, 16 * step + 16)
            low = slice(128 + 16 * step, 144 + 16 * step)
            for k in range(4):
                Y[half, k, top, cols] = (e[k][0] + t[k][0]).astype(bf16)
                Y[half, k, low, cols] = (e[k][1] + t[k][1]).astype(bf16)
                Y[half, k + 4, top, cols] = (e[k][0] - t[k][0]).astype(bf16)
                Y[half, k + 4, low, cols] = (e[k][1] - t[k][1]).astype(bf16)

    scale = ANGLES ** (-0.5)

    def spectrum(half, groups, beside, steps):
        first = 96 * groups[0]
        end = 96 if groups[-1] == 0 else 256
        for kk in steps:
            boths = [
                lax.dot_general(tab[k, first:end, :], Y[half, k], NT, preferred_element_type=f32)
                for k in (2 * kk, 2 * kk + 1)]
            for group in groups:
                lo, hi, size = ((0, 3, 48), (3, 8, 80))[group]
                top = 96 * group - first
                cosines = [both[top:top + size] for both in boths]
                sines = [both[top + size:top + 2 * size] for both in boths]
                res = [(c[:, :128] + n[:, 128:]) * scale for c, n in zip(cosines, sines)]
                ims = [(c[:, 128:] - n[:, :128]) * scale for c, n in zip(cosines, sines)]
                for t, parts in enumerate((res, ims)):
                    val = jnp.concatenate([p.reshape(size // 8, 8, 128) for p in parts], axis=1)
                    val = val.reshape(hi - lo, 2, 16, 128)
                    fst[half, lo:hi, kk, t] = val[:, 0]
                    stg[half, lo:hi, kk, t] = val[:, 1].astype(bf16)
            if beside is not None:
                combine(beside, kk)

    def to(src, dst, send, recv, target):
        return pltpu.make_async_remote_copy(
            src, dst, send, recv, device_id={"pulse": target}, device_id_type=MESH)

    def pair(half, group):
        lo, size = ((0, 3), (3, 5))[group]
        return to(stg.at[half, pl.ds(lo, size)], prx.at[half, pl.ds(lo, size)],
                  pair_s.at[half, group], pair_r.at[half, group], buddy)

    def near_copy(half, n):
        return to(zsn.at[half, 1 + n], near.at[half, n],
                  near_s.at[half, n], near_r.at[half, n], z_peer((1, 7)[n]))

    def far_copy(half, n):
        return to(zsn.at[half, 0, :, n], far.at[half, n],
                  far_s.at[half, n], far_r.at[half, n], z_peer((2, 6)[n]))

    def z_copy(half, n):
        return to(zsn.at[half, (5, 6, 4, 7)[n]], zrx.at[half, n],
                  z_s.at[half, n], z_r.at[half, n], z_peer((2, 6, 1, 7)[n]))

    def relay(half):
        pair(half, 0).wait()
        for q in range(3):
            zsn[half, q] = (fst[half, q] + prx[half, q].astype(f32)).astype(bf16)
        for n in range(2):
            far_copy(half, n).start()
        for n in range(2):
            near_copy(half, n).start()

    def scatter(half):
        pair(half, 1).wait()
        for n in (2, 3):
            q = (5, 6, 4, 7)[n]
            zsn[half, q] = (fst[half, q] + prx[half, q].astype(f32)).astype(bf16)
            z_copy(half, n).start()
        fst[half, 3] = fst[half, 3] + prx[half, 3].astype(f32)
        for n in (0, 1):
            far_copy(half, n).wait()
            near_copy(half, n).wait()
            q = 5 + n
            for t in range(2):
                both = fst[half, q, :, t] + prx[half, q, :, t].astype(f32) + near[half, n, :, t].astype(f32)
                if t == n:
                    both = both + far[half, n].astype(f32)
                zsn[half, q, :, t] = both.astype(bf16)
            z_copy(half, n).start()

    last(0)
    rotate_all(acc.at[0], 6, X.at[slot_of(1)], f32)
    table(7)
    rotate(acc.at[1], 7, 0, X.at[slot_of(3)], f32, 0, 128)
    last(1)
    for nt in range(4):
        combine(0, nt)
    rotate(acc.at[1], 7, 1, X.at[slot_of(3)], f32, 256, 384)
    spectrum(0, (0, 1), 1, range(4))
    pair(0, 0).start()
    pair(0, 1).start()
    spectrum(1, (0,), None, range(4))
    pair(1, 0).start()
    relay(0)
    spectrum(1, (1,), None, range(2))
    relay(1)
    spectrum(1, (1,), None, range(2, 4))
    pair(1, 1).start()
    scatter(0)
    scatter(1)

    for half in range(2):
        total = fst[half, 3]
        for n in (2, 3, 0, 1):
            z_copy(half, n).wait()
            total = total + zrx[half, n].astype(f32)
        for kk in range(4):
            for t in range(2):
                G[64 * t + 16 * kk:64 * t + 16 * kk + 16, 128 * half:128 * half + 128] = total[kk, t]

    gg = G[...]
    m = lax.dot_general(gg, gg, NT, precision=lax.Precision.HIGHEST, preferred_element_type=f32)
    lane = lax.broadcasted_iota(jnp.int32, (64, 128), 1)
    row = lax.broadcasted_iota(jnp.int32, (64, 128), 0)
    sign = jnp.where(lane < 64, 1.0, -1.0).astype(f32)
    cov = m[:64] * sign + pltpu.roll(m[64:], 64, 1)
    packed = jnp.where(lane <= row, cov, pltpu.roll(cov, 64, 1))
    packed = jnp.where(lane[:32] < 64, packed[:32], pltpu.roll(packed[32:], 64, 1))

    cx[ranged] = packed
    copies = []
    for k in (10, 9, 11, 6, 14, 2, 8, 5, 7, 13, 15, 1, 3, 4, 12):
        copy = pltpu.make_async_remote_copy(
            cx.at[ranged], cx.at[ranged], c_s.at[k - 1], c_r.at[k - 1],
            device_id={"range": r_peer(k)}, device_id_type=MESH)
        copy.start()
        copies.append(copy)
    for copy in copies:
        copy.wait()
    sums = [cx[n] for n in range(16)]
    while len(sums) > 1:
        sums = [sums[n] + sums[n + 1] for n in range(0, len(sums), 2)]
    packed = jnp.concatenate([sums[0], pltpu.roll(sums[0], 64, 1)], axis=0)
    square = jnp.concatenate([packed, packed], axis=0)
    flip = square.T[:64]
    c_re = jnp.where(lane <= row, packed, flip)
    c_im = jnp.where(lane > row, packed, jnp.where(lane < row, -flip, 0.0))

    K = jnp.concatenate([
        jnp.where(lane < 64, c_re, -pltpu.roll(c_im, 64, 1)),
        jnp.where(lane < 64, c_im, pltpu.roll(c_re, 64, 1)),
    ], axis=0)
    wide = lax.broadcasted_iota(jnp.int32, (128, 128), 1)
    w = jnp.sum(jnp.where(wide < 64, K, 0.0), axis=1, keepdims=True)
    v = w / jnp.sqrt(jnp.sum(w * w, axis=0, keepdims=True) + EPSILON)
    w = jnp.sum(K * v, axis=0, keepdims=True)
    v = w / jnp.sqrt(jnp.sum(w * w, axis=1, keepdims=True) + EPSILON)
    w = jnp.sum(K * v, axis=1, keepdims=True)
    v = w / jnp.sqrt(jnp.sum(w * w, axis=0, keepdims=True) + EPSILON)
    v = v * math.sqrt(BLOCK)
    vr = v[:64]
    vi = v[64:]
    gr = gg[:64]
    gi = gg[64:]
    focused = (gr * vr + gi * vi, gi * vr - gr * vi)
    for t in range(2):
        for k in range(8):
            for half in range(2):
                F[t, half, pl.ds(k, 8, stride=8), :] = focused[t][8 * k:8 * k + 8, 128 * half:128 * half + 128]
        for half in range(2):
            out[t, :, 128 * half:128 * half + 128] = F[t, half]


def per_device(pulse_data, merge_taps, merge_weights, squint):
    vmem = pl.BlockSpec(memory_space=pltpu.VMEM)
    dma = pltpu.SemaphoreType.DMA
    return pl.pallas_call(
        kernel,
        out_shape=jax.ShapeDtypeStruct((2, BLOCK, COLS), f32),
        in_specs=[pl.BlockSpec(memory_space=pl.ANY)] + [vmem] * 3,
        out_specs=vmem,
        scratch_shapes=[
            pltpu.VMEM((2, BEAMS, COLS), bf16),
            pltpu.VMEM((2, 512, BEAMS), bf16),
            pltpu.VMEM((8, 16, BEAMS), bf16),
            pltpu.VMEM((2, 16, BEAMS), bf16),
            pltpu.VMEM((2, BEAMS, BEAMS), bf16),
            pltpu.VMEM((256, 256), bf16),
            pltpu.VMEM((8, 2, 2, 8, BEAMS), f32),
            pltpu.VMEM((8, 2, 8, BEAMS), f32),
            pltpu.VMEM((2, 512, BEAMS), f32),
            pltpu.VMEM((512, BEAMS), bf16),
            pltpu.VMEM((2, 512, BEAMS), bf16),
            pltpu.VMEM((4, 512, BEAMS), f32),
            pltpu.VMEM((2, 8, 256, BEAMS), bf16),
            pltpu.VMEM((2, 16, BEAMS), f32),
            pltpu.VMEM((8, 256, BEAMS), bf16),
            pltpu.VMEM((2, 8, 4, 2, 16, 128), f32),
            pltpu.VMEM((2, 8, 4, 2, 16, 128), bf16),
            pltpu.VMEM((2, 8, 4, 2, 16, 128), bf16),
            pltpu.VMEM((2, 8, 4, 2, 16, 128), bf16),
            pltpu.VMEM((2, 2, 4, 2, 16, 128), bf16),
            pltpu.VMEM((2, 2, 4, 16, 128), bf16),
            pltpu.VMEM((2, 4, 4, 2, 16, 128), bf16),
            pltpu.VMEM((128, COLS), f32),
            pltpu.VMEM((2, 2, 64, 128), f32),
            pltpu.VMEM((16, 32, 128), f32),
            dma, dma, dma,
            dma((4,)), dma((4,)),
            dma((2, 2)), dma((2, 2)),
            dma((2, 2)), dma((2, 2)),
            dma((2, 2)), dma((2, 2)),
            dma((2, 4)), dma((2, 4)),
            dma((15,)), dma((15,)),
        ],
        compiler_params=pltpu.CompilerParams(
            collective_id=0, has_side_effects=True, vmem_limit_bytes=60 * 1024 * 1024),
    )(pulse_data, merge_taps, merge_weights, squint)


def solution(mesh):
    placed = (
        P(None, "pulse", "range"),
        P(None, None, None, "pulse"),
        P(None, None, None, "pulse"),
        P(None, "pulse"),
    )
    return jax.shard_map(
        per_device, mesh=mesh, in_specs=placed, out_specs=P(None, "pulse", "range"), check_vma=False
    )
```

```python
import math

import jax
import jax.numpy as jnp
from jax import lax
from jax.experimental import pallas as pl
from jax.experimental.pallas import tpu as pltpu
from jax.sharding import PartitionSpec as P

RANGES = 4096
ANGLES = 16384
BEAMS = 1024
COLS = 256
BLOCK = 64
EPSILON = 1e-06
TWO_PI = 2.0 * math.pi
COS_TERMS = [(-1) ** k * TWO_PI ** (2 * k) / math.factorial(2 * k) for k in range(10)]
SIN_TERMS = [(-1) ** k * TWO_PI ** (2 * k + 1) / math.factorial(2 * k + 1) for k in range(9)]
MESH = pl.DeviceIdType.MESH
f32 = jnp.float32
bf16 = jnp.bfloat16
NT = (((1,), (1,)), ((), ()))
STEPS = (4, 3, 5, 0, 1, 2, 6, 7)


def flipped(index, bit):
    return index + bit - 2 * bit * ((index // bit) % 2)


def sincos(turns):
    part = turns - jnp.floor(turns + 0.5)
    y = part * part
    c = jnp.full_like(y, COS_TERMS[-1])
    for term in COS_TERMS[-2::-1]:
        c = c * y + term
    s = jnp.full_like(y, SIN_TERMS[-1])
    for term in SIN_TERMS[-2::-1]:
        s = s * y + term
    return c, s * part


def kernel(
    data_hbm, taps, weights, squint, out,
    data, dT, prm, snd, W, rowid, rb, rs, acc, S1, U, X, Y, us, tab,
    fst, stg, prx, zsn, near, far, zrx, G, F, cx,
    load_s, part_s, part_r, prm_s, prm_r, pair_s, pair_r,
    near_s, near_r, far_s, far_r, z_s, z_r, c_s, c_r,
):
    pulse = lax.axis_index("pulse")
    ranged = lax.axis_index("range")
    z = pulse // 2
    core = pulse % 2
    gx = ranged // 4
    gy = ranged % 4
    other = 1 - core
    buddy = flipped(pulse, 1)
    q2 = flipped(pulse, 2)
    q4 = flipped(pulse, 4)
    q6 = flipped(q2, 4)

    def z_peer(k):
        return ((z + k) % 8) * 2 + core

    def r_peer(k):
        return ((gx + k // 4) % 4) * 4 + (gy + k % 4) % 4

    load = pltpu.make_async_copy(data_hbm, data, load_s)
    load.start()

    barrier = pltpu.get_barrier_semaphore()
    pl.semaphore_signal(barrier, inc=1, device_id={"pulse": buddy}, device_id_type=MESH)
    pl.semaphore_signal(barrier, inc=1, device_id={"pulse": q6}, device_id_type=MESH)
    for k in (1, 2, 6, 7):
        pl.semaphore_signal(barrier, inc=1, device_id={"pulse": z_peer(k)}, device_id_type=MESH)
    for k in range(1, 16):
        pl.semaphore_signal(barrier, inc=1, device_id={"range": r_peer(k)}, device_id_type=MESH)

    def fill(ref, level, source):
        tap = taps[level, source]
        slope = squint[level:level + 1, :]
        first = slope.astype(bf16).astype(f32)
        second = (slope - first).astype(bf16).astype(f32)
        third = slope - first - second
        ref[...] = jnp.concatenate([
            (tap % 256).astype(f32), (tap // 256).astype(f32), weights[level, source].astype(f32),
            first, second, third, jnp.zeros_like(slope)], axis=0).astype(bf16)

    fill(snd.at[0], 1, 1)
    fill(snd.at[1], 2, 1)
    fill(prm.at[4], 2, 0)
    fill(prm.at[0], 0, 0)
    fill(prm.at[1], 0, 1)
    fill(prm.at[2], 1, 0)
    rowid[...] = lax.broadcasted_iota(jnp.int32, (256, 256), 0).astype(f32).astype(bf16)

    def build(m, slot):
        for nt in range(4):
            cols = slice(256 * nt, 256 * nt + 256)
            rows = prm[m, :, cols].astype(f32)
            places = [rows[tap:tap + 1] + 256.0 * rows[4 + tap:5 + tap] for tap in range(4)]
            scales = [rows[8 + tap:9 + tap].astype(bf16) for tap in range(4)]
            for kb in range(4):
                val = jnp.zeros((256, 256), bf16)
                for tap in range(4):
                    here = rowid[...] == (places[tap] - 256.0 * kb).astype(bf16)
                    val = jnp.where(here, scales[tap], val)
                W[slot, 256 * kb:256 * kb + 256, cols] = val

    first_range = (ranged * COLS).astype(f32)

    def prepare_rotation(m):
        rows = prm[m].astype(f32)
        slope = rows[12:13] + rows[13:14] + rows[14:15]
        i8 = lax.broadcasted_iota(jnp.int32, (8, BEAMS), 0).astype(f32)
        c0, s0 = sincos(slope * ((i8 + first_range) * (1.0 / RANGES)))
        cf, sf = sincos(slope * (jnp.where(i8 < 1.0, 8.0, 128.0) * (1.0 / RANGES)))
        rb[m, 0, 0] = c0
        rb[m, 0, 1] = s0
        ch = cf[1:2]
        sh = sf[1:2]
        rb[m, 1, 0] = c0 * ch - s0 * sh
        rb[m, 1, 1] = s0 * ch + c0 * sh
        rs[m, 0] = jnp.broadcast_to(cf[0:1], (8, BEAMS))
        rs[m, 1] = jnp.broadcast_to(sf[0:1], (8, BEAMS))

    def rotate(src, m, half, dest, kind, re_at, im_at):
        for nt in range(4):
            cols = slice(256 * nt, 256 * nt + 256)
            c = rb[m, half, 0, :, cols]
            s = rb[m, half, 1, :, cols]
            c8 = rs[m, 0, :, cols]
            s8 = rs[m, 1, :, cols]
            for i in range(8):
                reals = []
                imags = []
                for e in range(2):
                    q = 16 * i + 8 * e
                    a = src[re_at + q:re_at + q + 8, cols]
                    b = src[im_at + q:im_at + q + 8, cols]
                    reals.append(c * a - s * b)
                    imags.append(s * a + c * b)
                    c, s = c * c8 - s * s8, s * c8 + c * s8
                q = 128 * half + 16 * i
                dest[q:q + 16, cols] = jnp.concatenate(reals, axis=0).astype(kind)
                dest[256 + q:272 + q, cols] = jnp.concatenate(imags, axis=0).astype(kind)

    def rotate_all(src, m, dest, kind):
        for half in range(2):
            rotate(src, m, half, dest, kind, 128 * half, 256 + 128 * half)

    first_angle = BEAMS * (core + 8 * (z // 4))

    def table_base():
        angle = lax.broadcasted_iota(jnp.int32, (1, BEAMS), 1) + first_angle
        rows = []
        for step in STEPS:
            for c in (core, other):
                rows.append(angle * (64 * (((z + step) % 8) * 2 + c)))
        us[0], us[1] = sincos((jnp.concatenate(rows, axis=0) % ANGLES).astype(f32) * (1.0 / ANGLES))

    def table(k):
        a8 = lax.broadcasted_iota(jnp.int32, (8, BEAMS), 1) + first_angle
        v8 = 8 * lax.broadcasted_iota(jnp.int32, (8, BEAMS), 0) + k
        vc, vs = sincos(((v8 * a8) % ANGLES).astype(f32) * (1.0 / ANGLES))
        for q in range(8):
            cs = []
            ss = []
            for u in (2 * q, 2 * q + 1):
                uc = us[0, u:u + 1, :]
                un = us[1, u:u + 1, :]
                cs.append(uc * vc - un * vs)
                ss.append(un * vc + uc * vs)
            at_c, at_s = (16 * q, 48 + 16 * q) if q < 3 else (48 + 16 * q, 128 + 16 * q)
            tab[k, at_c:at_c + 16, :] = jnp.concatenate(cs, axis=0).astype(bf16)
            tab[k, at_s:at_s + 16, :] = jnp.concatenate(ss, axis=0).astype(bf16)

    build(0, 0)

    load.wait()
    for t in range(2):
        dT[0, t * COLS:(t + 1) * COLS, :] = data[t].T

    pl.semaphore_wait(barrier, 21)

    part = pltpu.make_async_remote_copy(
        dT.at[0], dT.at[1], part_s, part_r, device_id={"pulse": buddy}, device_id_type=MESH)
    part.start()
    prm_copies = []
    for n, (src, slot, target) in enumerate((
        (snd.at[0], 3, q2), (snd.at[1], 5, q4), (prm.at[4], 6, q2), (snd.at[1], 7, q6))):
        copy = pltpu.make_async_remote_copy(
            src, prm.at[slot], prm_s.at[n], prm_r.at[n],
            device_id={"pulse": target}, device_id_type=MESH)
        copy.start()
        prm_copies.append(copy)

    acc[0] = jnp.dot(dT[0], W[0], preferred_element_type=f32)
    build(1, 1)
    prepare_rotation(0)
    table_base()
    prepare_rotation(2)
    table(0)
    part.wait()
    acc[1] = jnp.dot(dT[1], W[1], preferred_element_type=f32) + acc[0]
    build(2, 0)
    table(1)
    rotate_all(acc.at[1], 0, S1, bf16)

    acc[0] = jnp.dot(S1[...], W[0], preferred_element_type=f32)
    prm_copies[0].wait()
    build(3, 1)
    prepare_rotation(3)
    table(2)

    acc[1] = jnp.dot(S1[...], W[1], preferred_element_type=f32)
    build(4, 0)
    rotate_all(acc.at[0], 2, U.at[0], bf16)
    prepare_rotation(4)
    table(3)

    bit0 = z % 2
    bit1 = (z // 2) % 2

    def slot_of(i):
        at0 = bit0 if i % 2 == 0 else 1 - bit0
        at1 = bit1 if i // 2 == 0 else 1 - bit1
        return at0 + 2 * at1

    acc[0] = jnp.dot(U[0], W[0], preferred_element_type=f32)
    prm_copies[1].wait()
    build(5, 1)
    rotate_all(acc.at[1], 3, U.at[1], bf16)
    prepare_rotation(5)
    table(4)

    acc[1] = jnp.dot(U[0], W[1], preferred_element_type=f32)
    prm_copies[2].wait()
    build(6, 0)
    rotate_all(acc.at[0], 4, X.at[slot_of(0)], f32)
    prepare_rotation(6)
    table(5)

    acc[0] = jnp.dot(U[1], W[0], preferred_element_type=f32)
    prm_copies[3].wait()
    build(7, 1)
    rotate_all(acc.at[1], 5, X.at[slot_of(2)], f32)
    prepare_rotation(7)
    table(6)

    def last(half):
        lhs = jnp.concatenate(
            [U[1, 128 * half:128 * half + 128, :], U[1, 256 + 128 * half:384 + 128 * half, :]], axis=0)
        acc[1, 256 * half:256 * half + 256, :] = jnp.dot(lhs, W[1], preferred_element_type=f32)

    root = math.sqrt(0.5)

    def combine(half, nt):
        cols = slice(256 * nt, 256 * nt + 256)
        for step in range(8):
            top = slice(128 * half + 16 * step, 128 * half + 16 * step + 16)
            low = slice(256 + 128 * half + 16 * step, 272 + 128 * half + 16 * step)
            xr = [X[n, top, cols] for n in range(4)]
            xi = [X[n, low, cols] for n in range(4)]
            e = [
                (xr[0] + xr[2], xi[0] + xi[2]),
                (xr[0] + xi[2], xi[0] - xr[2]),
                (xr[0] - xr[2], xi[0] - xi[2]),
                (xr[0] - xi[2], xi[0] + xr[2]),
            ]
            o = [
                (xr[1] + xr[3], xi[1] + xi[3]),
                (xr[1] + xi[3], xi[1] - xr[3]),
                (xr[1] - xr[3], xi[1] - xi[3]),
                (xr[1] - xi[3], xi[1] + xr[3]),
            ]
            t = [
                o[0],
                (root * (o[1][0] + o[1][1]), root * (o[1][1] - o[1][0])),
                (o[2][1], -o[2][0]),
                (root * (o[3][1] - o[3][0]), -root * (o[3][0] + o[3][1])),
            ]
            top = slice(16 * step, 16 * step + 16)
            low = slice(128 + 16 * step, 144 + 16 * step)
            for k in range(4):
                Y[half, k, top, cols] = (e[k][0] + t[k][0]).astype(bf16)
                Y[half, k, low, cols] = (e[k][1] + t[k][1]).astype(bf16)
                Y[half, k + 4, top, cols] = (e[k][0] - t[k][0]).astype(bf16)
                Y[half, k + 4, low, cols] = (e[k][1] - t[k][1]).astype(bf16)

    scale = ANGLES ** (-0.5)

    def spectrum(half, groups, beside, steps):
        first = 96 * groups[0]
        end = 96 if groups[-1] == 0 else 256
        for kk in steps:
            boths = [
                lax.dot_general(tab[k, first:end, :], Y[half, k], NT, preferred_element_type=f32)
                for k in (2 * kk, 2 * kk + 1)]
            for group in groups:
                lo, hi, size = ((0, 3, 48), (3, 8, 80))[group]
                top = 96 * group - first
                cosines = [both[top:top + size] for both in boths]
                sines = [both[top + size:top + 2 * size] for both in boths]
                res = [(c[:, :128] + n[:, 128:]) * scale for c, n in zip(cosines, sines)]
                ims = [(c[:, 128:] - n[:, :128]) * scale for c, n in zip(cosines, sines)]
                for t, parts in enumerate((res, ims)):
                    val = jnp.concatenate([p.reshape(size // 8, 8, 128) for p in parts], axis=1)
                    val = val.reshape(hi - lo, 2, 16, 128)
                    fst[half, lo:hi, kk, t] = val[:, 0]
                    stg[half, lo:hi, kk, t] = val[:, 1].astype(bf16)
            if beside is not None:
                combine(beside, kk)

    def to(src, dst, send, recv, target):
        return pltpu.make_async_remote_copy(
            src, dst, send, recv, device_id={"pulse": target}, device_id_type=MESH)

    def pair(half, group):
        lo, size = ((0, 3), (3, 5))[group]
        return to(stg.at[half, pl.ds(lo, size)], prx.at[half, pl.ds(lo, size)],
                  pair_s.at[half, group], pair_r.at[half, group], buddy)

    def near_copy(half, n):
        return to(zsn.at[half, 1 + n], near.at[half, n],
                  near_s.at[half, n], near_r.at[half, n], z_peer((1, 7)[n]))

    def far_copy(half, n):
        return to(zsn.at[half, 0, :, n], far.at[half, n],
                  far_s.at[half, n], far_r.at[half, n], z_peer((2, 6)[n]))

    def z_copy(half, n):
        return to(zsn.at[half, (5, 6, 4, 7)[n]], zrx.at[half, n],
                  z_s.at[half, n], z_r.at[half, n], z_peer((2, 6, 1, 7)[n]))

    def relay(half):
        pair(half, 0).wait()
        for q in range(3):
            zsn[half, q] = (fst[half, q] + prx[half, q].astype(f32)).astype(bf16)
        for n in range(2):
            far_copy(half, n).start()
        for n in range(2):
            near_copy(half, n).start()

    def direct(half):
        pair(half, 1).wait()
        for n in (2, 3):
            q = (5, 6, 4, 7)[n]
            zsn[half, q] = (fst[half, q] + prx[half, q].astype(f32)).astype(bf16)
            z_copy(half, n).start()
        fst[half, 3] = fst[half, 3] + prx[half, 3].astype(f32)

    def scatter(half):
        for n in (0, 1):
            far_copy(half, n).wait()
            near_copy(half, n).wait()
            q = 5 + n
            for t in range(2):
                both = fst[half, q, :, t] + prx[half, q, :, t].astype(f32) + near[half, n, :, t].astype(f32)
                if t == n:
                    both = both + far[half, n].astype(f32)
                zsn[half, q, :, t] = both.astype(bf16)
            z_copy(half, n).start()

    last(0)
    rotate_all(acc.at[0], 6, X.at[slot_of(1)], f32)
    table(7)
    rotate(acc.at[1], 7, 0, X.at[slot_of(3)], f32, 0, 128)
    last(1)
    for nt in range(4):
        combine(0, nt)
    rotate(acc.at[1], 7, 1, X.at[slot_of(3)], f32, 256, 384)
    spectrum(0, (0, 1), 1, range(4))
    pair(0, 0).start()
    pair(0, 1).start()
    spectrum(1, (0,), None, range(4))
    pair(1, 0).start()
    relay(0)
    direct(0)
    spectrum(1, (1,), None, range(2))
    relay(1)
    spectrum(1, (1,), None, range(2, 4))
    pair(1, 1).start()
    scatter(0)
    direct(1)
    scatter(1)

    for half in range(2):
        total = fst[half, 3]
        for n in (2, 3, 0, 1):
            z_copy(half, n).wait()
            total = total + zrx[half, n].astype(f32)
        for kk in range(4):
            for t in range(2):
                G[64 * t + 16 * kk:64 * t + 16 * kk + 16, 128 * half:128 * half + 128] = total[kk, t]

    gg = G[...]
    m = lax.dot_general(gg, gg, NT, precision=lax.Precision.HIGHEST, preferred_element_type=f32)
    lane = lax.broadcasted_iota(jnp.int32, (64, 128), 1)
    row = lax.broadcasted_iota(jnp.int32, (64, 128), 0)
    sign = jnp.where(lane < 64, 1.0, -1.0).astype(f32)
    cov = m[:64] * sign + pltpu.roll(m[64:], 64, 1)
    packed = jnp.where(lane <= row, cov, pltpu.roll(cov, 64, 1))
    packed = jnp.where(lane[:32] < 64, packed[:32], pltpu.roll(packed[32:], 64, 1))

    cx[ranged] = packed
    copies = []
    for k in (10, 9, 11, 6, 14, 2, 8, 5, 7, 13, 15, 1, 3, 4, 12):
        copy = pltpu.make_async_remote_copy(
            cx.at[ranged], cx.at[ranged], c_s.at[k - 1], c_r.at[k - 1],
            device_id={"range": r_peer(k)}, device_id_type=MESH)
        copy.start()
        copies.append(copy)
    for copy in copies:
        copy.wait()
    sums = [cx[n] for n in range(16)]
    while len(sums) > 1:
        sums = [sums[n] + sums[n + 1] for n in range(0, len(sums), 2)]
    packed = jnp.concatenate([sums[0], pltpu.roll(sums[0], 64, 1)], axis=0)
    square = jnp.concatenate([packed, packed], axis=0)
    flip = square.T[:64]
    c_re = jnp.where(lane <= row, packed, flip)
    c_im = jnp.where(lane > row, packed, jnp.where(lane < row, -flip, 0.0))

    K = jnp.concatenate([
        jnp.where(lane < 64, c_re, -pltpu.roll(c_im, 64, 1)),
        jnp.where(lane < 64, c_im, pltpu.roll(c_re, 64, 1)),
    ], axis=0)
    wide = lax.broadcasted_iota(jnp.int32, (128, 128), 1)
    w = jnp.sum(jnp.where(wide < 64, K, 0.0), axis=1, keepdims=True)
    v = w / jnp.sqrt(jnp.sum(w * w, axis=0, keepdims=True) + EPSILON)
    w = jnp.sum(K * v, axis=0, keepdims=True)
    v = w / jnp.sqrt(jnp.sum(w * w, axis=1, keepdims=True) + EPSILON)
    w = jnp.sum(K * v, axis=1, keepdims=True)
    v = w / jnp.sqrt(jnp.sum(w * w, axis=0, keepdims=True) + EPSILON)
    v = v * math.sqrt(BLOCK)
    vr = v[:64]
    vi = v[64:]
    gr = gg[:64]
    gi = gg[64:]
    focused = (gr * vr + gi * vi, gi * vr - gr * vi)
    for t in range(2):
        for k in range(8):
            for half in range(2):
                F[t, half, pl.ds(k, 8, stride=8), :] = focused[t][8 * k:8 * k + 8, 128 * half:128 * half + 128]
        for half in range(2):
            out[t, :, 128 * half:128 * half + 128] = F[t, half]


def per_device(pulse_data, merge_taps, merge_weights, squint):
    vmem = pl.BlockSpec(memory_space=pltpu.VMEM)
    dma = pltpu.SemaphoreType.DMA
    return pl.pallas_call(
        kernel,
        out_shape=jax.ShapeDtypeStruct((2, BLOCK, COLS), f32),
        in_specs=[pl.BlockSpec(memory_space=pl.ANY)] + [vmem] * 3,
        out_specs=vmem,
        scratch_shapes=[
            pltpu.VMEM((2, BEAMS, COLS), bf16),
            pltpu.VMEM((2, 512, BEAMS), bf16),
            pltpu.VMEM((8, 16, BEAMS), bf16),
            pltpu.VMEM((2, 16, BEAMS), bf16),
            pltpu.VMEM((2, BEAMS, BEAMS), bf16),
            pltpu.VMEM((256, 256), bf16),
            pltpu.VMEM((8, 2, 2, 8, BEAMS), f32),
            pltpu.VMEM((8, 2, 8, BEAMS), f32),
            pltpu.VMEM((2, 512, BEAMS), f32),
            pltpu.VMEM((512, BEAMS), bf16),
            pltpu.VMEM((2, 512, BEAMS), bf16),
            pltpu.VMEM((4, 512, BEAMS), f32),
            pltpu.VMEM((2, 8, 256, BEAMS), bf16),
            pltpu.VMEM((2, 16, BEAMS), f32),
            pltpu.VMEM((8, 256, BEAMS), bf16),
            pltpu.VMEM((2, 8, 4, 2, 16, 128), f32),
            pltpu.VMEM((2, 8, 4, 2, 16, 128), bf16),
            pltpu.VMEM((2, 8, 4, 2, 16, 128), bf16),
            pltpu.VMEM((2, 8, 4, 2, 16, 128), bf16),
            pltpu.VMEM((2, 2, 4, 2, 16, 128), bf16),
            pltpu.VMEM((2, 2, 4, 16, 128), bf16),
            pltpu.VMEM((2, 4, 4, 2, 16, 128), bf16),
            pltpu.VMEM((128, COLS), f32),
            pltpu.VMEM((2, 2, 64, 128), f32),
            pltpu.VMEM((16, 32, 128), f32),
            dma, dma, dma,
            dma((4,)), dma((4,)),
            dma((2, 2)), dma((2, 2)),
            dma((2, 2)), dma((2, 2)),
            dma((2, 2)), dma((2, 2)),
            dma((2, 4)), dma((2, 4)),
            dma((15,)), dma((15,)),
        ],
        compiler_params=pltpu.CompilerParams(
            collective_id=0, has_side_effects=True, vmem_limit_bytes=60 * 1024 * 1024),
    )(pulse_data, merge_taps, merge_weights, squint)


def solution(mesh):
    placed = (
        P(None, "pulse", "range"),
        P(None, None, None, "pulse"),
        P(None, None, None, "pulse"),
        P(None, "pulse"),
    )
    return jax.shard_map(
        per_device, mesh=mesh, in_specs=placed, out_specs=P(None, "pulse", "range"), check_vma=False
    )
```
